32 devices in a mesh: parts: 2 (over y), seq: 4 (over z), dp: 2 (over x), fsdp: 2 (over core).
Axes of the slice: x: 2, y: 2, z: 4, core: 2. Of those that a mesh axis runs over, the one named last changes fastest.
Arguments:
- inputs: bfloat16 [8, 960, 1024], P(('parts', 'dp', 'fsdp'), 'seq'), parts along dimension 0, may hold values from -6 to 6
- conv_weight: bfloat16 [4096, 128], P(('seq', 'dp', 'fsdp')), may hold values from -0.25 to 0.25
- score_weight: bfloat16 [1024], P(('seq', 'dp', 'fsdp')), may hold values from -0.375 to 0.375
- lengths: int32 [8], P(('parts', 'dp', 'fsdp')), parts along dimension 0, may hold values from 480 to 960, as said below
- offsets: int32 [8, 16], P(('parts', 'dp', 'fsdp')), parts along dimension 0, may hold values from 0 to 956, as said below
- cotangent: bfloat16 [8, 480, 1024], P(('parts', 'dp', 'fsdp'), 'seq'), parts along dimension 0, may hold values from -6 to 6
Outputs:
- x_grad: bfloat16 [8, 960, 1024], P(('parts', 'dp', 'fsdp'), 'seq'), parts along dimension 0
- conv_grad: float32 [8192, 128], P(('parts', 'seq', 'dp', 'fsdp')), parts along dimension 0
- score_grad: float32 [2048], P(('parts', 'seq', 'dp', 'fsdp')), parts along dimension 0
The draws below stay inside these ranges and needn't reach their ends.
There are 2 independent parts, one for each index of `parts`. The reference program is written for one: setup_inputs(seed, part) draws one part's arguments, and reference() takes and returns one part's arrays. A program takes and returns all parts, laid end to end along the dimension named above; an argument that names none is the same for every part. Nothing has to cross between parts.
Inputs may be any that keep to these rules, and one draw needn't show every extreme that they name: `lengths`: each length is a multiple of 4; one stream in every draw uses all 960 characters. In each stream the first offset is 0, the offsets rise strictly, and each is a multiple of 4.
All inputs are finite; a program needn't handle non-finite values.
Results may differ from the reference program's by a relative error of at most 0.0049.
Values may be sent and summed in bfloat16 or wider, within the bound.
No kernel may reach another device: no remote copies, remote signals or barrier semaphores. Data moves between devices by JAX's collectives and lax.ppermute only.
A program may use at most 64 MiB of HBM per device.

```python
import jax
import jax.numpy as jnp
from jax import lax

D = 1024
GROUPS = 8
KERNEL = 4
GROUP_WIDTH = 128
FILES = 16
LENGTH = 960
SEQS = 4


def draw_lengths(key, part):
    first_key, second_key = jax.random.split(key)
    quarters = jax.random.randint(first_key, (SEQS,), LENGTH // 8, LENGTH // 4 + 1)
    chosen = jax.random.randint(second_key, (), 0, SEQS)
    stream_ids = jnp.arange(SEQS)
    shortest = (chosen + 1) % SEQS
    drawn = jnp.where(stream_ids == shortest, LENGTH // 8 * 4, quarters * 4)
    return jnp.where(stream_ids == chosen, LENGTH, drawn).astype(jnp.int32)


def draw_offsets(key, part):
    stream_keys = jax.random.split(jax.random.fold_in(key, 7), SEQS)

    def one_stream(stream_key):
        picked = jax.random.permutation(stream_key, LENGTH // 4 - 2)[:FILES - 2]
        starts = (jnp.sort(picked) + 1) * 4
        last_start = jnp.full((1,), LENGTH - 4, jnp.int32)
        return jnp.concatenate([jnp.zeros((1,), jnp.int32), starts.astype(jnp.int32), last_start])
    return jax.vmap(one_stream)(stream_keys)


def block_scale(rng, extent, shards, least, high):
    def one(position, shards_of):
        steps = jax.random.uniform(jax.random.fold_in(jax.random.fold_in(rng, 6), position), (shards_of,), jnp.float32, least / len(shards), high / len(shards))
        return jnp.repeat(jnp.exp(steps), extent[position] // shards_of).reshape((-1,) + (1,) * (len(extent) - position - 1))

    gain = one(*shards[0])
    for cut in shards[1:]:
        gain = gain * one(*cut)
    return gain


def centred(key, extent, spread, limit, cuts=(), kind=jnp.bfloat16):
    values = jax.random.normal(key, extent, jnp.float32) * spread
    if len(cuts) > 0:
        values = block_scale(key, extent, cuts, -0.22, 0.18) * values
    return jnp.clip(values, min=-limit, max=limit).astype(kind)


def setup_inputs(seed: int = 0, part: int = 0) -> dict:
    key_list = jax.random.split(jax.random.key(seed), 7)
    part_keys = jax.random.split(jax.random.fold_in(key_list[6], part), 7)
    inputs = centred(part_keys[0], (SEQS, LENGTH, D), 1.0, 6.0, ((0, 4), (1, 4)))
    conv_weight = centred(key_list[1], (GROUPS * KERNEL * GROUP_WIDTH, GROUP_WIDTH), (KERNEL * GROUP_WIDTH) ** -0.5, 0.25, ((0, 16),))
    score_weight = centred(key_list[2], (D,), (D // 4) ** -0.5, 0.375, ((0, 16),))
    lengths = draw_lengths(jax.random.fold_in(jax.random.fold_in(key_list[6], part), 71), part)
    offsets = draw_offsets(jax.random.fold_in(jax.random.fold_in(key_list[6], part), 71), part)
    cotangent = centred(part_keys[5], (SEQS, LENGTH // 2, D), 1.0, 6.0, ((0, 4), (1, 4)))
    return dict(inputs=inputs, conv_weight=conv_weight, score_weight=score_weight, lengths=lengths, offsets=offsets, cotangent=cotangent)


precise_mode = lax.Precision.HIGHEST


def segment_of(positions, offsets):
    return jnp.sum((offsets[None, :] <= positions[:, None]).astype(jnp.int32), axis=1)


def tap_valid(positions, offsets, lag_steps):
    earlier = positions - lag_steps
    same_file = segment_of(positions, offsets) == segment_of(earlier, offsets)
    return jnp.logical_and(earlier >= 0, same_file)


def mix_backward(hidden, upstream, score_vec):
    row_count = hidden.shape[0]
    width_all = hidden.shape[1]
    pooled_list = []
    logit_list = []
    for block_size in range(1, 5):
        pooled = hidden.reshape(row_count // block_size, block_size, width_all).sum(axis=1) * (1.0 / block_size)
        pooled_list.append(pooled)
        logit_list.append(jnp.repeat(jnp.dot(pooled, score_vec, precision=precise_mode), block_size))
    logits = jnp.stack(logit_list)
    exp_logits = jnp.exp(logits)
    choose_prob = exp_logits / jnp.sum(exp_logits, axis=0)
    mix_grad = jnp.repeat(upstream.astype(jnp.float32) * 0.5, 2, axis=0)
    inner_list = []
    for block_size in range(1, 5):
        pooled = pooled_list[block_size - 1]
        inner = jnp.sum(mix_grad.reshape(row_count // block_size, block_size, width_all) * pooled[:, None, :], axis=2)
        inner_list.append(inner.reshape(row_count))
    inner_all = jnp.stack(inner_list)
    dlogit = choose_prob * (inner_all - jnp.sum(choose_prob * inner_all, axis=0))
    hidden_grad = jnp.zeros((row_count, width_all), jnp.float32)
    weight_grad = jnp.zeros((width_all,), jnp.float32)
    for block_size in range(1, 5):
        block_logit = dlogit[block_size - 1].reshape(row_count // block_size, block_size).sum(axis=1)
        block_mix = (choose_prob[block_size - 1][:, None] * mix_grad).reshape(row_count // block_size, block_size, width_all).sum(axis=1)
        block_term = (block_mix + block_logit[:, None] * score_vec[None, :]) * (1.0 / block_size)
        hidden_grad = hidden_grad + jnp.repeat(block_term, block_size, axis=0)
        weight_grad = weight_grad + jnp.dot(block_logit, pooled_list[block_size - 1], precision=precise_mode)
    return hidden_grad, weight_grad


def stream_grads(stream_rows, length_one, file_starts, upstream, conv_weight, score_weight):
    total_rows = stream_rows.shape[0]
    positions = jnp.arange(total_rows, dtype=jnp.int32)
    valid = (positions < length_one).astype(jnp.float32)
    padded = jnp.concatenate([jnp.zeros((KERNEL - 1, D), stream_rows.dtype), stream_rows], axis=0)
    tap_list = []
    for tap_index in range(KERNEL):
        window = padded[KERNEL - 1 - tap_index:KERNEL - 1 - tap_index + total_rows]
        keep = tap_valid(positions, file_starts, tap_index)
        tap_list.append(jnp.where(keep[:, None], window, jnp.zeros_like(window)))
    taps = jnp.stack(tap_list, axis=1).reshape(total_rows, KERNEL, GROUPS, GROUP_WIDTH)
    kernel_full = conv_weight.reshape(GROUPS, KERNEL, GROUP_WIDTH, GROUP_WIDTH).astype(jnp.float32)
    hidden = jnp.einsum("nkgc,gkco->ngo", taps.astype(jnp.float32), kernel_full).reshape(total_rows, D) * valid[:, None]
    hidden_grad, weight_grad = mix_backward(hidden, upstream, score_weight.astype(jnp.float32))
    hidden_low = (hidden_grad * valid[:, None]).astype(jnp.bfloat16)
    grad_padded = jnp.concatenate([hidden_low, jnp.zeros((KERNEL - 1, D), jnp.bfloat16)], axis=0)
    grad_list = []
    for tap_index in range(KERNEL):
        window = grad_padded[tap_index:tap_index + total_rows]
        keep = tap_valid(positions + tap_index, file_starts, tap_index)
        grad_list.append(jnp.where(keep[:, None], window, jnp.zeros_like(window)))
    grad_taps = jnp.stack(grad_list, axis=1).reshape(total_rows, KERNEL, GROUPS, GROUP_WIDTH)
    input_grad = jnp.einsum("nkgo,gkco->ngc", grad_taps.astype(jnp.float32), kernel_full).reshape(total_rows, D).astype(jnp.bfloat16)
    kernel_grad = jnp.einsum("nkgc,ngo->gkco", taps.astype(jnp.float32), hidden_low.reshape(total_rows, GROUPS, GROUP_WIDTH).astype(jnp.float32))
    return input_grad, kernel_grad.reshape(GROUPS * KERNEL * GROUP_WIDTH, GROUP_WIDTH), weight_grad


def reference(inputs, conv_weight, score_weight, lengths, offsets, cotangent):
    def one_stream(packed):
        return stream_grads(packed[0], packed[1], packed[2], packed[3], conv_weight, score_weight)

    results = lax.map(one_stream, (inputs, lengths, offsets, cotangent))
    return results[0], jnp.sum(results[1], axis=0), jnp.sum(results[2], axis=0)
```

```python
import functools

import jax
import jax.numpy as jnp
from jax import lax
from jax.experimental import pallas as pl
from jax.experimental.pallas import tpu as pltpu
from jax.sharding import PartitionSpec as P

GROUPS = 8
KERNEL = 4
GROUP_WIDTH = 128


precise_mode = lax.Precision.HIGHEST


def shifted(value, axis, by):
    devices = lax.axis_size(axis)
    pairs = [(i, i + by) for i in range(devices) if 0 <= i + by < devices]
    return lax.ppermute(value, axis, pairs)


def segment_of(positions, offsets):
    return jnp.sum((offsets[None, :] <= positions[:, None]).astype(jnp.int32), axis=1)


def tap_valid(positions, offsets, lag_steps):
    earlier = positions - lag_steps
    same_file = segment_of(positions, offsets) == segment_of(earlier, offsets)
    return jnp.logical_and(earlier >= 0, same_file)


def mix_backward(hidden, upstream, score_vec):
    row_count = hidden.shape[0]
    width_all = hidden.shape[1]
    pooled_list = []
    logit_list = []
    for block_size in range(1, 5):
        pooled = hidden.reshape(row_count // block_size, block_size, width_all).sum(axis=1) * (
            1.0 / block_size
        )
        pooled_list.append(pooled)
        logit_list.append(
            jnp.repeat(jnp.dot(pooled, score_vec, precision=precise_mode), block_size)
        )
    logits = jnp.stack(logit_list)
    exp_logits = jnp.exp(logits)
    choose_prob = exp_logits / jnp.sum(exp_logits, axis=0)
    mix_grad = jnp.repeat(upstream.astype(jnp.float32) * 0.5, 2, axis=0)
    inner_list = []
    for block_size in range(1, 5):
        pooled = pooled_list[block_size - 1]
        inner = jnp.sum(
            mix_grad.reshape(row_count // block_size, block_size, width_all) * pooled[:, None, :],
            axis=2,
        )
        inner_list.append(inner.reshape(row_count))
    inner_all = jnp.stack(inner_list)
    dlogit = choose_prob * (inner_all - jnp.sum(choose_prob * inner_all, axis=0))
    hidden_grad = jnp.zeros((row_count, width_all), jnp.float32)
    weight_grad = jnp.zeros((width_all,), jnp.float32)
    for block_size in range(1, 5):
        block_logit = (
            dlogit[block_size - 1].reshape(row_count // block_size, block_size).sum(axis=1)
        )
        block_mix = (
            (choose_prob[block_size - 1][:, None] * mix_grad)
            .reshape(row_count // block_size, block_size, width_all)
            .sum(axis=1)
        )
        block_term = (block_mix + block_logit[:, None] * score_vec[None, :]) * (1.0 / block_size)
        hidden_grad = hidden_grad + jnp.repeat(block_term, block_size, axis=0)
        weight_grad = weight_grad + jnp.dot(
            block_logit, pooled_list[block_size - 1], precision=precise_mode
        )
    return (hidden_grad, weight_grad)


def per_device_general(inputs, conv_weight, score_weight, lengths, offsets, cotangent):
    local_rows = inputs.shape[1]
    width_all = inputs.shape[2]
    kernel_flat, score_full = (
        lax.all_gather(conv_weight, ("seq", "dp", "fsdp"), axis=0, tiled=True),
        lax.all_gather(score_weight, ("seq", "dp", "fsdp"), axis=0, tiled=True),
    )
    kernel_full = kernel_flat.reshape(GROUPS, KERNEL, GROUP_WIDTH, GROUP_WIDTH)
    score_vec = score_full.astype(jnp.float32)
    start_row = lax.axis_index("seq") * local_rows
    positions = start_row + jnp.arange(local_rows, dtype=jnp.int32)
    own_rows = inputs[0]
    file_starts = offsets[0]
    valid = (positions < lengths[0]).astype(jnp.float32)
    left_rows = shifted(own_rows[local_rows - (KERNEL - 1) :], "seq", 1)
    padded = jnp.concatenate([left_rows, own_rows], axis=0)
    windows = []
    hidden = jnp.zeros((local_rows, GROUPS, GROUP_WIDTH), jnp.float32)
    for tap_index in range(KERNEL):
        window = padded[KERNEL - 1 - tap_index : KERNEL - 1 - tap_index + local_rows]
        keep = tap_valid(positions, file_starts, tap_index)
        window = jnp.where(keep[:, None], window, jnp.zeros_like(window)).reshape(
            local_rows, GROUPS, GROUP_WIDTH
        )
        windows.append(window)
        hidden = hidden + jnp.einsum(
            "ngc,gco->ngo", window, kernel_full[:, tap_index], preferred_element_type=jnp.float32
        )
    hidden = hidden.reshape(local_rows, width_all) * valid[:, None]
    hidden_grad, weight_grad = mix_backward(hidden, cotangent[0], score_vec)
    hidden_low = (hidden_grad * valid[:, None]).astype(jnp.bfloat16)
    right_rows = shifted(hidden_low[: KERNEL - 1], "seq", -1)
    grad_padded = jnp.concatenate([hidden_low, right_rows], axis=0)
    hidden_groups = hidden_low.reshape(local_rows, GROUPS, GROUP_WIDTH)
    input_grad = jnp.zeros((local_rows, GROUPS, GROUP_WIDTH), jnp.float32)
    kernel_terms = []
    for tap_index in range(KERNEL):
        window = grad_padded[tap_index : tap_index + local_rows]
        keep = tap_valid(positions + tap_index, file_starts, tap_index)
        window = jnp.where(keep[:, None], window, jnp.zeros_like(window)).reshape(
            local_rows, GROUPS, GROUP_WIDTH
        )
        input_grad = input_grad + jnp.einsum(
            "ngo,gco->ngc", window, kernel_full[:, tap_index], preferred_element_type=jnp.float32
        )
        kernel_terms.append(
            jnp.einsum(
                "ngc,ngo->gco",
                windows[tap_index],
                hidden_groups,
                preferred_element_type=jnp.float32,
            )
        )
    input_grad = input_grad.reshape(local_rows, width_all).astype(jnp.bfloat16)[None]
    kernel_part = jnp.stack(kernel_terms, axis=1).reshape(
        GROUPS * KERNEL * GROUP_WIDTH, GROUP_WIDTH
    )
    kernel_grad, score_grad = (
        lax.psum_scatter(kernel_part, ("seq", "dp", "fsdp"), scatter_dimension=0, tiled=True),
        lax.psum_scatter(weight_grad, ("seq", "dp", "fsdp"), scatter_dimension=0, tiled=True),
    )
    return (input_grad, kernel_grad, score_grad)


SLOTS = 4
HALF = SLOTS * GROUP_WIDTH
PAD = 8
SCORE_ROW = 2 * GROUP_WIDTH
HALO_ROW = SCORE_ROW + 16
BF = jnp.bfloat16
F32 = jnp.float32


def lanes(slot):
    return slice(slot * GROUP_WIDTH, (slot + 1) * GROUP_WIDTH)


def group_lanes(group):
    return pl.ds(pl.multiple_of(group * GROUP_WIDTH, GROUP_WIDTH), GROUP_WIDTH)


def slot_group(seq, slot, parity):
    return 2 * lax.rem(seq - slot + 2 * SLOTS, SLOTS) + parity


def call(body, out_shape, scratch=(), smem=0, cost=None):
    def run(*args):
        specs = [pl.BlockSpec(memory_space=pltpu.SMEM)] * smem
        specs += [pl.BlockSpec(memory_space=pltpu.VMEM)] * (len(args) - smem)
        return pl.pallas_call(
            body,
            out_shape=out_shape,
            in_specs=specs,
            out_specs=jax.tree.map(lambda _: pl.BlockSpec(memory_space=pltpu.VMEM), out_shape),
            scratch_shapes=list(scratch),
            cost_estimate=cost,
            compiler_params=pltpu.CompilerParams(vmem_limit_bytes=48 * 1024 * 1024),
        )(*args)

    return run


def pack_kernel(off_ref, len_ref, x_ref, c_ref, w_ref, score_ref, mx, mc, mw, mw1, md):
    rows = x_ref.shape[1]
    pairs = c_ref.shape[1]
    s, d, f = (lax.axis_index(name) for name in ("seq", "dp", "fsdp"))
    for j in range(SLOTS):
        col = group_lanes(slot_group(s, j, 1 - d))
        mx[:, lanes(j)] = x_ref[0, :, col]
        mc[0:pairs, lanes(j)] = c_ref[0, :, col]
        next_other = group_lanes(slot_group(s + 1, j, 1 - d))
        md[:, lanes(j)] = x_ref[0, rows - PAD :, next_other]
        next_own = group_lanes(slot_group(s + 1, j, d))
        mw1[HALO_ROW + PAD * j : HALO_ROW + PAD * (j + 1), :] = x_ref[0, rows - PAD :, next_own]
    lane = lax.broadcasted_iota(jnp.int32, (PAD, GROUP_WIDTH), 1)
    start = s * rows
    info = jnp.zeros((PAD, GROUP_WIDTH), jnp.int32)
    for i in range(off_ref.shape[1]):
        info = jnp.where(lane == i, jnp.clip(off_ref[0, i] - start, -4, rows + PAD), info)
    info = jnp.where(lane == off_ref.shape[1], jnp.clip(len_ref[0] - start, 0, rows), info)
    mc[pairs:, :] = jnp.zeros((mc.shape[0] - pairs, HALF), BF)
    mc[pairs : pairs + PAD, lanes(0)] = (info.astype(F32) * 0.25).astype(BF)
    value = score_ref[...].astype(F32)
    both = jnp.concatenate([value, value], axis=1)
    half = lax.broadcasted_iota(jnp.int32, (16, GROUP_WIDTH), 1) // (GROUP_WIDTH // 2)
    row = lax.broadcasted_iota(jnp.int32, (16, GROUP_WIDTH), 0)
    block = jnp.where((half == f) & (row == 0), jnp.broadcast_to(both, (16, GROUP_WIDTH)), 0.0)
    for ref in (mw, mw1):
        ref[0:SCORE_ROW, :] = w_ref[...]
        ref[SCORE_ROW:HALO_ROW, :] = block.astype(BF)


def row_info(mc_ref, pairs, files, extent):
    info = mc_ref[pairs : pairs + PAD, lanes(0)].astype(F32)[0:1] * 4.0
    lane = lax.broadcasted_iota(jnp.int32, (1, GROUP_WIDTH), 1)
    length = jnp.sum(jnp.where(lane == files, info, 0.0), axis=1, keepdims=True)
    pos = lax.broadcasted_iota(jnp.int32, (extent, GROUP_WIDTH), 0).astype(F32)
    starts = jnp.where((lane < files) & (info <= pos), info, -4096.0)
    since = pos - jnp.max(starts, axis=1, keepdims=True)
    return since, (pos < length).astype(F32)


def block_weights(rows):
    q = lax.broadcasted_iota(jnp.int32, (rows, GROUP_WIDTH), 0)
    r = lax.broadcasted_iota(jnp.int32, (rows, GROUP_WIDTH), 1)

    def over(value, size):
        if size == 1:
            return value
        if size == 3:
            return lax.shift_right_logical(value * 21846, 16)
        return lax.shift_right_logical(value, size // 2)

    return [
        [
            jnp.where(over(q, size) == over(2 * r + odd, size), 1.0 / size, 0.0).astype(F32)
            for size in range(1, 5)
        ]
        for odd in range(2)
    ]


def windows_of(tail, rows_value, since):
    rows = rows_value.shape[0]
    padded = jnp.concatenate([tail.astype(F32), rows_value.astype(F32)], axis=0)
    out = [rows_value]
    for lag in range(1, KERNEL):
        moved = pltpu.roll(padded, lag, 0)[PAD:]
        out.append(jnp.where(since[:rows] >= lag, moved, 0.0).astype(BF))
    return out


def stream_parts(x_ref, mx_ref, w1_ref, md_ref, j, stream):
    s, d = lax.axis_index("seq"), lax.axis_index("dp")
    if stream == 0:
        return (
            w1_ref[HALO_ROW + PAD * j : HALO_ROW + PAD * (j + 1), :],
            x_ref[0, :, group_lanes(slot_group(s, j, d))],
        )
    return md_ref[:, lanes(j)], mx_ref[:, lanes(j)]


def kernel_halves(w_refs, j):
    f = lax.axis_index("fsdp")
    mine, theirs = w_refs[j][0:SCORE_ROW, :], w_refs[SLOTS + j][0:SCORE_ROW, :]
    first = jnp.full((SCORE_ROW, GROUP_WIDTH), f, jnp.int32) == 0
    return jnp.where(first, mine, theirs), jnp.where(first, theirs, mine)


def nt(a, b):
    return lax.dot_general(a, b, (((1,), (1,)), ((), ())), preferred_element_type=F32)


def two_terms(value):
    high = value.astype(BF)
    return high, (value - high.astype(F32)).astype(BF)


def hidden_kernel(files, x_ref, c_ref, mx_ref, mc_ref, mcr_ref, md_ref, *refs):
    w_refs, (h_out, l_out, r_out) = refs[: 2 * SLOTS], refs[2 * SLOTS :]
    rows, pairs = x_ref.shape[1], c_ref.shape[1]
    s, d = lax.axis_index("seq"), lax.axis_index("dp")
    infos = [row_info(ref, pairs, files, rows) for ref in (mc_ref, mcr_ref)]
    gram = [jnp.zeros((rows, GROUP_WIDTH), F32) for _ in range(2)]
    for j in range(SLOTS):
        low, high = kernel_halves(w_refs, j)
        score = (
            w_refs[j][SCORE_ROW:HALO_ROW, :].astype(F32)
            + w_refs[SLOTS + j][SCORE_ROW:HALO_ROW, :].astype(F32)
        )[0:PAD]
        for stream in range(2):
            since, valid = infos[stream]
            tail, value = stream_parts(x_ref, mx_ref, w_refs[1], md_ref, j, stream)
            win = windows_of(tail, value, since)
            hidden = jnp.dot(
                jnp.concatenate(win[:2], axis=1), low, preferred_element_type=F32
            ) + jnp.dot(jnp.concatenate(win[2:], axis=1), high, preferred_element_type=F32)
            hidden = hidden * valid
            h_out[stream, :, lanes(j)] = hidden
            if stream == 0:
                cot = c_ref[0, :, group_lanes(slot_group(s, j, d))]
            else:
                cot = mcr_ref[0:pairs, lanes(j)]
            left = jnp.concatenate([cot.astype(F32), score], axis=0).astype(BF)
            l_out[stream, :, lanes(j)] = left
            a, b = two_terms(hidden)
            gram[stream] = gram[stream] + nt(a, left) + nt(b, left)
    weights = block_weights(rows)
    for stream in range(2):
        column = gram[stream][:, pairs : pairs + 1]
        inner = [
            jnp.sum(weights[odd][b] * gram[stream], axis=0, keepdims=True) * 0.5
            for odd in range(2)
            for b in range(4)
        ]
        logit = [
            jnp.sum(weights[odd][b] * column, axis=0, keepdims=True)
            for odd in range(2)
            for b in range(4)
        ]
        r_out[stream] = jnp.concatenate(inner + logit, axis=0)


def mix_kernel(files, x_ref, mx_ref, md_ref, w1_ref, mc_ref, mcr_ref, h_ref, l_ref, r_ref, rr_ref,
               hg_out, hh_out, mine_out, send_out):
    rows = x_ref.shape[1]
    pairs = rows // 2
    f = lax.axis_index("fsdp")
    weights = block_weights(rows)
    infos = [row_info(ref, pairs, files, rows) for ref in (mc_ref, mcr_ref)]
    lane = lax.broadcasted_iota(jnp.int32, (rows, GROUP_WIDTH), 1)
    columns = []
    for stream in range(2):
        total = r_ref[stream] + rr_ref[1 - stream]
        spread = jnp.zeros((rows, GROUP_WIDTH), F32)
        carry = jnp.zeros((rows, GROUP_WIDTH), F32)
        for odd in range(2):
            inner = [total[4 * odd + b : 4 * odd + b + 1] for b in range(4)]
            logit = [total[8 + 4 * odd + b : 8 + 4 * odd + b + 1] for b in range(4)]
            top = jnp.maximum(jnp.maximum(logit[0], logit[1]), jnp.maximum(logit[2], logit[3]))
            powers = [jnp.exp(v - top) for v in logit]
            scale = 1.0 / (powers[0] + powers[1] + powers[2] + powers[3])
            choose = [v * scale for v in powers]
            mean = sum(c * m for c, m in zip(choose, inner))
            for b in range(4):
                spread = spread + weights[odd][b] * (choose[b] * 0.5)
                carry = carry + weights[odd][b] * (choose[b] * (inner[b] - mean))
        valid = infos[stream][1]
        e = jnp.sum(carry, axis=1, keepdims=True)
        columns.append(e)
        mixed = jnp.where(lane == pairs, e, spread) * valid
        a, b = two_terms(mixed)
        for j in range(SLOTS):
            left = l_ref[stream, :, lanes(j)]
            grad = jnp.dot(a, left, preferred_element_type=F32) + jnp.dot(
                b, left, preferred_element_type=F32
            )
            grad = grad.astype(BF)
            hg_out[stream, :, lanes(j)] = grad
            hh_out[PAD * stream : PAD * (stream + 1), lanes((j + SLOTS - 1) % SLOTS)] = grad[0:PAD]
    first = jnp.full((SCORE_ROW, GROUP_WIDTH), f, jnp.int32) == 0
    row = lax.broadcasted_iota(jnp.int32, (PAD, GROUP_WIDTH), 0)
    for j in range(SLOTS):
        low = jnp.zeros((SCORE_ROW, GROUP_WIDTH), F32)
        high = jnp.zeros((SCORE_ROW, GROUP_WIDTH), F32)
        score = jnp.zeros((1, GROUP_WIDTH), F32)
        for stream in range(2):
            tail, value = stream_parts(x_ref, mx_ref, w1_ref, md_ref, j, stream)
            win = windows_of(tail, value, infos[stream][0])
            grad = hg_out[stream, :, lanes(j)]
            dims = (((0,), (0,)), ((), ()))
            low = low + lax.dot_general(
                jnp.concatenate(win[:2], axis=1), grad, dims, preferred_element_type=F32
            )
            high = high + lax.dot_general(
                jnp.concatenate(win[2:], axis=1), grad, dims, preferred_element_type=F32
            )
            score = score + jnp.sum(
                columns[stream] * h_ref[stream, :, lanes(j)], axis=0, keepdims=True
            )
        base = j * (SCORE_ROW + PAD)
        score = jnp.where(row == 0, jnp.broadcast_to(score, row.shape), 0.0)
        mine_out[base : base + SCORE_ROW, :] = jnp.where(first, low, high)
        send_out[base : base + SCORE_ROW, :] = jnp.where(first, high, low)
        mine_out[base + SCORE_ROW : base + SCORE_ROW + PAD, :] = score
        send_out[base + SCORE_ROW : base + SCORE_ROW + PAD, :] = score


def add_kernel(mine_ref, got_ref, *outs):
    for j, out in zip(range(1, SLOTS), outs):
        base = j * (SCORE_ROW + PAD)
        total = mine_ref[base : base + SCORE_ROW + PAD, :] + got_ref[base : base + SCORE_ROW + PAD, :]
        out[0:SCORE_ROW, :] = total[0:SCORE_ROW].astype(BF)
        a, b = two_terms(total[SCORE_ROW:])
        out[SCORE_ROW:, :] = jnp.concatenate([a.astype(F32), b.astype(F32)], axis=0).astype(BF)


def sum_kernel(mine_ref, got_ref, z1, z2, z3, out_ref, score_ref):
    f = lax.axis_index("fsdp")
    total = mine_ref[0 : SCORE_ROW + PAD, :] + got_ref[0 : SCORE_ROW + PAD, :]
    grad, score = total[0:SCORE_ROW], total[SCORE_ROW:]
    for ref in (z1, z2, z3):
        grad = grad + ref[0:SCORE_ROW, :].astype(F32)
        pair = ref[SCORE_ROW:, :].astype(F32)
        score = score + pair[0:PAD] + pair[PAD:]
    out_ref[...] = grad
    half = GROUP_WIDTH // 2
    score_ref[...] = jnp.where(
        jnp.full((1, half), f, jnp.int32) == 0, score[0:1, :half], score[0:1, half:]
    )


def input_kernel(files, hg_ref, hh_ref, mc_ref, mcr_ref, *refs):
    w_refs, outs = refs[: 2 * SLOTS], refs[2 * SLOTS :]
    rows = hg_ref.shape[1]
    pairs = rows // 2
    for stream, mref in enumerate((mc_ref, mcr_ref)):
        since, _ = row_info(mref, pairs, files, rows + PAD)
        for j in range(SLOTS):
            padded = jnp.concatenate(
                [
                    hg_ref[stream, :, lanes(j)].astype(F32),
                    hh_ref[PAD * stream : PAD * (stream + 1), lanes(j)].astype(F32),
                ],
                axis=0,
            )
            halves = kernel_halves(w_refs, j)
            total = jnp.zeros((rows, GROUP_WIDTH), F32)
            for lag in range(KERNEL):
                if lag == 0:
                    window = padded[:rows].astype(BF)
                else:
                    kept = jnp.where(since >= lag, padded, 0.0)
                    window = pltpu.roll(kept, rows + PAD - lag, 0)[:rows].astype(BF)
                part = halves[lag // 2][GROUP_WIDTH * (lag % 2) : GROUP_WIDTH * (lag % 2 + 1)]
                total = total + nt(window, part)
            outs[stream][:, lanes(j)] = total.astype(BF)


def place_kernel(own_ref, got_ref, out_ref):
    s, d = lax.axis_index("seq"), lax.axis_index("dp")
    for j in range(SLOTS):
        out_ref[0, :, group_lanes(slot_group(s, j, d))] = own_ref[:, lanes(j)]
        out_ref[0, :, group_lanes(slot_group(s, j, 1 - d))] = got_ref[:, lanes(j)]


def per_device_paired(inputs, conv_weight, score_weight, lengths, offsets, cotangent):
    rows, pairs, files = inputs.shape[1], cotangent.shape[1], offsets.shape[1]
    shape = jax.ShapeDtypeStruct

    def flip(value, axis):
        return lax.ppermute(value, axis, [(0, 1), (1, 0)])

    def cycle(value, by):
        return lax.ppermute(value, "seq", [(i, (i + by) % SLOTS) for i in range(SLOTS)])

    def across(value, by):
        pairs_of = [
            (i * 2 + j, (i + by) * 2 + 1 - j)
            for i in range(SLOTS)
            for j in range(2)
            if 0 <= i + by < SLOTS
        ]
        return lax.ppermute(value, ("seq", "dp"), pairs_of)

    wide = HALO_ROW + PAD * SLOTS
    mx, mc, mw, mw1, md = call(
        pack_kernel,
        (
            shape((rows, HALF), BF),
            shape((pairs + PAD, HALF), BF),
            shape((HALO_ROW, GROUP_WIDTH), BF),
            shape((wide, GROUP_WIDTH), BF),
            shape((PAD, HALF), BF),
        ),
        smem=2,
    )(offsets, lengths, inputs, cotangent, conv_weight, score_weight.reshape(1, -1))
    mxr = flip(mx, "dp")
    shards = [mw, cycle(mw1, 1), cycle(mw, 2), cycle(mw, 3)]
    mcr = flip(mc, "dp")
    mdr = across(md, 1)
    shards = shards + [flip(w, "fsdp") for w in shards]
    hidden, left, partial = call(
        functools.partial(hidden_kernel, files),
        (
            shape((2, rows, HALF), F32),
            shape((2, pairs + PAD, HALF), BF),
            shape((2, 16, GROUP_WIDTH), F32),
        ),
    )(inputs, cotangent, mxr, mc, mcr, mdr, *shards)
    partial_r = flip(partial, "dp")
    grad_rows = SLOTS * (SCORE_ROW + PAD)
    hg, hh, mine, send = call(
        functools.partial(mix_kernel, files),
        (
            shape((2, rows, HALF), BF),
            shape((2 * PAD, HALF), BF),
            shape((grad_rows, GROUP_WIDTH), F32),
            shape((grad_rows, GROUP_WIDTH), F32),
        ),
    )(inputs, mxr, mdr, shards[1], mc, mcr, hidden, left, partial, partial_r)
    hhr = shifted(hh, "seq", -1)
    got = flip(send, "fsdp")
    sums = call(add_kernel, tuple(shape((HALO_ROW, GROUP_WIDTH), BF) for _ in range(SLOTS - 1)))(
        mine, got
    )
    x_own, x_send = call(
        functools.partial(input_kernel, files),
        (shape((rows, HALF), BF), shape((rows, HALF), BF)),
    )(hg, hhr, mc, mcr, *shards)
    x_got = flip(x_send, "dp")
    final = [cycle(value, -j) for j, value in zip(range(1, SLOTS), sums)]
    input_grad = call(place_kernel, shape(inputs.shape, BF))(x_own, x_got)
    kernel_grad, score_grad = call(
        sum_kernel,
        (shape((SCORE_ROW, GROUP_WIDTH), F32), shape((1, GROUP_WIDTH // 2), F32)),
    )(mine, got, *final)
    return (input_grad, kernel_grad, score_grad.reshape(-1))


def solution(mesh):
    placed = (
        P(("parts", "dp", "fsdp"), "seq", None),
        P(("seq", "dp", "fsdp"), None),
        P(("seq", "dp", "fsdp")),
        P(("parts", "dp", "fsdp")),
        P(("parts", "dp", "fsdp"), None),
        P(("parts", "dp", "fsdp"), "seq", None),
    )
    paired = mesh.shape["seq"] == SLOTS and mesh.shape["dp"] == 2 and mesh.shape["fsdp"] == 2
    return jax.shard_map(
        per_device_paired if paired else per_device_general,
        mesh=mesh,
        in_specs=placed,
        out_specs=(
            P(("parts", "dp", "fsdp"), "seq", None),
            P(("parts", "seq", "dp", "fsdp"), None),
            P(("parts", "seq", "dp", "fsdp")),
        ),
        check_vma=False,
    )
```

```python
import functools

import jax
import jax.numpy as jnp
from jax import lax
from jax.experimental import pallas as pl
from jax.experimental.pallas import tpu as pltpu
from jax.sharding import PartitionSpec as P

GROUPS = 8
KERNEL = 4
GROUP_WIDTH = 128


precise_mode = lax.Precision.HIGHEST


def shifted(value, axis, by):
    devices = lax.axis_size(axis)
    pairs = [(i, i + by) for i in range(devices) if 0 <= i + by < devices]
    return lax.ppermute(value, axis, pairs)


def segment_of(positions, offsets):
    return jnp.sum((offsets[None, :] <= positions[:, None]).astype(jnp.int32), axis=1)


def tap_valid(positions, offsets, lag_steps):
    earlier = positions - lag_steps
    same_file = segment_of(positions, offsets) == segment_of(earlier, offsets)
    return jnp.logical_and(earlier >= 0, same_file)


def mix_backward(hidden, upstream, score_vec):
    row_count = hidden.shape[0]
    width_all = hidden.shape[1]
    pooled_list = []
    logit_list = []
    for block_size in range(1, 5):
        pooled = hidden.reshape(row_count // block_size, block_size, width_all).sum(axis=1) * (
            1.0 / block_size
        )
        pooled_list.append(pooled)
        logit_list.append(
            jnp.repeat(jnp.dot(pooled, score_vec, precision=precise_mode), block_size)
        )
    logits = jnp.stack(logit_list)
    exp_logits = jnp.exp(logits)
    choose_prob = exp_logits / jnp.sum(exp_logits, axis=0)
    mix_grad = jnp.repeat(upstream.astype(jnp.float32) * 0.5, 2, axis=0)
    inner_list = []
    for block_size in range(1, 5):
        pooled = pooled_list[block_size - 1]
        inner = jnp.sum(
            mix_grad.reshape(row_count // block_size, block_size, width_all) * pooled[:, None, :],
            axis=2,
        )
        inner_list.append(inner.reshape(row_count))
    inner_all = jnp.stack(inner_list)
    dlogit = choose_prob * (inner_all - jnp.sum(choose_prob * inner_all, axis=0))
    hidden_grad = jnp.zeros((row_count, width_all), jnp.float32)
    weight_grad = jnp.zeros((width_all,), jnp.float32)
    for block_size in range(1, 5):
        block_logit = (
            dlogit[block_size - 1].reshape(row_count // block_size, block_size).sum(axis=1)
        )
        block_mix = (
            (choose_prob[block_size - 1][:, None] * mix_grad)
            .reshape(row_count // block_size, block_size, width_all)
            .sum(axis=1)
        )
        block_term = (block_mix + block_logit[:, None] * score_vec[None, :]) * (1.0 / block_size)
        hidden_grad = hidden_grad + jnp.repeat(block_term, block_size, axis=0)
        weight_grad = weight_grad + jnp.dot(
            block_logit, pooled_list[block_size - 1], precision=precise_mode
        )
    return (hidden_grad, weight_grad)


def per_device_general(inputs, conv_weight, score_weight, lengths, offsets, cotangent):
    local_rows = inputs.shape[1]
    width_all = inputs.shape[2]
    kernel_flat, score_full = (
        lax.all_gather(conv_weight, ("seq", "dp", "fsdp"), axis=0, tiled=True),
        lax.all_gather(score_weight, ("seq", "dp", "fsdp"), axis=0, tiled=True),
    )
    kernel_full = kernel_flat.reshape(GROUPS, KERNEL, GROUP_WIDTH, GROUP_WIDTH)
    score_vec = score_full.astype(jnp.float32)
    start_row = lax.axis_index("seq") * local_rows
    positions = start_row + jnp.arange(local_rows, dtype=jnp.int32)
    own_rows = inputs[0]
    file_starts = offsets[0]
    valid = (positions < lengths[0]).astype(jnp.float32)
    left_rows = shifted(own_rows[local_rows - (KERNEL - 1) :], "seq", 1)
    padded = jnp.concatenate([left_rows, own_rows], axis=0)
    windows = []
    hidden = jnp.zeros((local_rows, GROUPS, GROUP_WIDTH), jnp.float32)
    for tap_index in range(KERNEL):
        window = padded[KERNEL - 1 - tap_index : KERNEL - 1 - tap_index + local_rows]
        keep = tap_valid(positions, file_starts, tap_index)
        window = jnp.where(keep[:, None], window, jnp.zeros_like(window)).reshape(
            local_rows, GROUPS, GROUP_WIDTH
        )
        windows.append(window)
        hidden = hidden + jnp.einsum(
            "ngc,gco->ngo", window, kernel_full[:, tap_index], preferred_element_type=jnp.float32
        )
    hidden = hidden.reshape(local_rows, width_all) * valid[:, None]
    hidden_grad, weight_grad = mix_backward(hidden, cotangent[0], score_vec)
    hidden_low = (hidden_grad * valid[:, None]).astype(jnp.bfloat16)
    right_rows = shifted(hidden_low[: KERNEL - 1], "seq", -1)
    grad_padded = jnp.concatenate([hidden_low, right_rows], axis=0)
    hidden_groups = hidden_low.reshape(local_rows, GROUPS, GROUP_WIDTH)
    input_grad = jnp.zeros((local_rows, GROUPS, GROUP_WIDTH), jnp.float32)
    kernel_terms = []
    for tap_index in range(KERNEL):
        window = grad_padded[tap_index : tap_index + local_rows]
        keep = tap_valid(positions + tap_index, file_starts, tap_index)
        window = jnp.where(keep[:, None], window, jnp.zeros_like(window)).reshape(
            local_rows, GROUPS, GROUP_WIDTH
        )
        input_grad = input_grad + jnp.einsum(
            "ngo,gco->ngc", window, kernel_full[:, tap_index], preferred_element_type=jnp.float32
        )
        kernel_terms.append(
            jnp.einsum(
                "ngc,ngo->gco",
                windows[tap_index],
                hidden_groups,
                preferred_element_type=jnp.float32,
            )
        )
    input_grad = input_grad.reshape(local_rows, width_all).astype(jnp.bfloat16)[None]
    kernel_part = jnp.stack(kernel_terms, axis=1).reshape(
        GROUPS * KERNEL * GROUP_WIDTH, GROUP_WIDTH
    )
    kernel_grad, score_grad = (
        lax.psum_scatter(kernel_part, ("seq", "dp", "fsdp"), scatter_dimension=0, tiled=True),
        lax.psum_scatter(weight_grad, ("seq", "dp", "fsdp"), scatter_dimension=0, tiled=True),
    )
    return (input_grad, kernel_grad, score_grad)


SLOTS = 4
HALF = SLOTS * GROUP_WIDTH
PAD = 8
SCORE_ROW = 2 * GROUP_WIDTH
HALO_ROW = SCORE_ROW + 16
BF = jnp.bfloat16
F32 = jnp.float32


def lanes(slot):
    return slice(slot * GROUP_WIDTH, (slot + 1) * GROUP_WIDTH)


def group_lanes(group):
    return pl.ds(pl.multiple_of(group * GROUP_WIDTH, GROUP_WIDTH), GROUP_WIDTH)


def slot_group(seq, slot, parity):
    return 2 * lax.rem(seq - slot + 2 * SLOTS, SLOTS) + parity


def call(body, out_shape, scratch=(), hbm=0):
    def run(*args):
        specs = [pl.BlockSpec(memory_space=pltpu.HBM)] * hbm
        specs += [pl.BlockSpec(memory_space=pltpu.VMEM)] * (len(args) - hbm)
        return pl.pallas_call(
            body,
            out_shape=out_shape,
            in_specs=specs,
            out_specs=jax.tree.map(lambda _: pl.BlockSpec(memory_space=pltpu.VMEM), out_shape),
            scratch_shapes=list(scratch),
            compiler_params=pltpu.CompilerParams(vmem_limit_bytes=48 * 1024 * 1024),
        )(*args)

    return run


def pack_kernel(off_hbm, x_hbm, c_hbm, w_hbm, score_hbm, len_ref, mine, other, mw, mw1, md,
                off_ref, x_ref, c_ref, score_ref, sems):
    rows, pairs, files = x_ref.shape[1], c_ref.shape[1], off_ref.shape[1]
    s, d, f = (lax.axis_index(name) for name in ("seq", "dp", "fsdp"))
    copies = [
        pltpu.make_async_copy(source, target, sems.at[i])
        for i, (source, target) in enumerate(
            (
                (x_hbm, x_ref),
                (c_hbm, c_ref),
                (off_hbm, off_ref),
                (score_hbm, score_ref),
                (w_hbm, mw.at[0:SCORE_ROW]),
                (w_hbm, mw1.at[0:SCORE_ROW]),
            )
        )
    ]
    for copy in copies:
        copy.start()
    for copy in copies[2:4]:
        copy.wait()
    lane = lax.broadcasted_iota(jnp.int32, (PAD, GROUP_WIDTH), 1)
    start = s * rows
    info = jnp.zeros((PAD, GROUP_WIDTH), jnp.int32)
    for i in range(files):
        info = jnp.where(lane == i, jnp.clip(off_ref[0, i] - start, -4, rows + PAD), info)
    info = jnp.where(lane == files, jnp.clip(len_ref[0:1, 0:1] - start, 0, rows), info)
    info = (info.astype(F32) * 0.25).astype(BF)
    value = score_ref[...].astype(F32)
    both = jnp.concatenate([value, value], axis=1)
    half = lax.broadcasted_iota(jnp.int32, (16, GROUP_WIDTH), 1) // (GROUP_WIDTH // 2)
    row = lax.broadcasted_iota(jnp.int32, (16, GROUP_WIDTH), 0)
    block = jnp.where((half == f) & (row == 0), jnp.broadcast_to(both, (16, GROUP_WIDTH)), 0.0)
    for ref in (mw, mw1):
        ref[SCORE_ROW:HALO_ROW, :] = block.astype(BF)
    copies[0].wait()
    for ref, parity in ((other, 1 - d), (mine, d)):
        for j in range(SLOTS):
            ref[0:rows, lanes(j)] = x_ref[0, :, group_lanes(slot_group(s, j, parity))]
    for j in range(SLOTS):
        next_other = group_lanes(slot_group(s + 1, j, 1 - d))
        md[:, lanes(j)] = x_ref[0, rows - PAD :, next_other]
        next_own = group_lanes(slot_group(s + 1, j, d))
        mw1[HALO_ROW + PAD * j : HALO_ROW + PAD * (j + 1), :] = x_ref[0, rows - PAD :, next_own]
    copies[1].wait()
    for ref, parity in ((other, 1 - d), (mine, d)):
        for j in range(SLOTS):
            col = group_lanes(slot_group(s, j, parity))
            ref[rows : rows + pairs, lanes(j)] = c_ref[0, :, col]
        ref[rows + pairs :, :] = jnp.zeros((PAD, HALF), BF)
        ref[rows + pairs :, lanes(0)] = info
    copies[4].wait()
    copies[5].wait()


def row_info(message, files):
    extent = (message.shape[0] - PAD) // 3 * 2
    info = message[message.shape[0] - PAD :, lanes(0)].astype(F32)[0:1] * 4.0
    lane = lax.broadcasted_iota(jnp.int32, (1, GROUP_WIDTH), 1)
    length = jnp.sum(jnp.where(lane == files, info, 0.0), axis=1, keepdims=True)
    pos = lax.broadcasted_iota(jnp.int32, (extent, GROUP_WIDTH), 0).astype(F32)
    starts = jnp.where((lane < files) & (info <= pos), info, -4096.0)
    since = pos - jnp.max(starts, axis=1, keepdims=True)
    return since, (pos < length).astype(F32)


def block_weights(rows):
    q = lax.broadcasted_iota(jnp.int32, (rows, GROUP_WIDTH), 0)
    r = lax.broadcasted_iota(jnp.int32, (rows, GROUP_WIDTH), 1)

    def over(value, size):
        if size == 1:
            return value
        if size == 3:
            return lax.shift_right_logical(value * 21846, 16)
        return lax.shift_right_logical(value, size // 2)

    return [
        [
            jnp.where(over(q, size) == over(2 * r + odd, size), 1.0 / size, 0.0).astype(F32)
            for size in range(1, 5)
        ]
        for odd in range(2)
    ]


def windows_of(tail, rows_value, since):
    rows = rows_value.shape[0]
    padded = jnp.concatenate([tail.astype(F32), rows_value.astype(F32)], axis=0)
    out = [rows_value]
    for lag in range(1, KERNEL):
        moved = pltpu.roll(padded, lag, 0)[PAD:]
        out.append(jnp.where(since >= lag, moved, 0.0).astype(BF))
    return out


def stream_parts(messages, w1_ref, md_ref, j, stream):
    rows = (messages[stream].shape[0] - PAD) // 3 * 2
    if stream == 0:
        tail = w1_ref[HALO_ROW + PAD * j : HALO_ROW + PAD * (j + 1), :]
    else:
        tail = md_ref[:, lanes(j)]
    return tail, messages[stream][0:rows, lanes(j)]


def kernel_halves(w_refs, j):
    f = lax.axis_index("fsdp")
    mine, theirs = w_refs[j][0:SCORE_ROW, :], w_refs[SLOTS + j][0:SCORE_ROW, :]
    first = jnp.full((SCORE_ROW, GROUP_WIDTH), f, jnp.int32) == 0
    return jnp.where(first, mine, theirs), jnp.where(first, theirs, mine)


def nt(a, b):
    return lax.dot_general(a, b, (((1,), (1,)), ((), ())), preferred_element_type=F32)


def two_terms(value):
    high = value.astype(BF)
    return high, (value - high.astype(F32)).astype(BF)


def hidden_kernel(files, mine_ref, other_ref, md_ref, *refs):
    w_refs, (h_out, l_out, r_out) = refs[: 2 * SLOTS], refs[2 * SLOTS :]
    messages = (mine_ref, other_ref)
    rows = h_out.shape[1]
    pairs = rows // 2
    infos = [row_info(ref, files) for ref in messages]
    gram = [jnp.zeros((rows, GROUP_WIDTH), F32) for _ in range(2)]
    for j in range(SLOTS):
        low, high = kernel_halves(w_refs, j)
        score = (
            w_refs[j][SCORE_ROW:HALO_ROW, :].astype(F32)
            + w_refs[SLOTS + j][SCORE_ROW:HALO_ROW, :].astype(F32)
        )[0:PAD]
        for stream in range(2):
            since, valid = infos[stream]
            tail, value = stream_parts(messages, w_refs[1], md_ref, j, stream)
            win = windows_of(tail, value, since)
            hidden = jnp.dot(
                jnp.concatenate(win[:2], axis=1), low, preferred_element_type=F32
            ) + jnp.dot(jnp.concatenate(win[2:], axis=1), high, preferred_element_type=F32)
            hidden = hidden * valid
            h_out[stream, :, lanes(j)] = hidden
            cot = messages[stream][rows : rows + pairs, lanes(j)]
            left = jnp.concatenate([cot.astype(F32), score], axis=0).astype(BF)
            l_out[stream, :, lanes(j)] = left
            a, b = two_terms(hidden)
            gram[stream] = gram[stream] + nt(a, left) + nt(b, left)
    weights = block_weights(rows)
    for stream in range(2):
        column = gram[stream][:, pairs : pairs + 1]
        inner = [
            jnp.sum(weights[odd][b] * gram[stream], axis=0, keepdims=True) * 0.5
            for odd in range(2)
            for b in range(4)
        ]
        logit = [
            jnp.sum(weights[odd][b] * column, axis=0, keepdims=True)
            for odd in range(2)
            for b in range(4)
        ]
        r_out[stream] = jnp.concatenate(inner + logit, axis=0)


def mix_kernel(files, mine_ref, other_ref, md_ref, w1_ref, h_ref, l_ref, r_ref, rr_ref,
               hg_out, mine_out, send_out):
    messages = (mine_ref, other_ref)
    rows = h_ref.shape[1]
    pairs = rows // 2
    f = lax.axis_index("fsdp")
    weights = block_weights(rows)
    infos = [row_info(ref, files) for ref in messages]
    lane = lax.broadcasted_iota(jnp.int32, (rows, GROUP_WIDTH), 1)
    columns = []
    for stream in range(2):
        total = r_ref[stream] + rr_ref[1 - stream]
        spread = jnp.zeros((rows, GROUP_WIDTH), F32)
        carry = jnp.zeros((rows, GROUP_WIDTH), F32)
        for odd in range(2):
            inner = [total[4 * odd + b : 4 * odd + b + 1] for b in range(4)]
            logit = [total[8 + 4 * odd + b : 8 + 4 * odd + b + 1] for b in range(4)]
            top = jnp.maximum(jnp.maximum(logit[0], logit[1]), jnp.maximum(logit[2], logit[3]))
            powers = [jnp.exp(v - top) for v in logit]
            scale = 1.0 / (powers[0] + powers[1] + powers[2] + powers[3])
            choose = [v * scale for v in powers]
            mean = sum(c * m for c, m in zip(choose, inner))
            for b in range(4):
                spread = spread + weights[odd][b] * (choose[b] * 0.5)
                carry = carry + weights[odd][b] * (choose[b] * (inner[b] - mean))
        valid = infos[stream][1]
        e = jnp.sum(carry, axis=1, keepdims=True)
        columns.append(e)
        mixed = jnp.where(lane == pairs, e, spread) * valid
        a, b = two_terms(mixed)
        for j in range(SLOTS):
            left = l_ref[stream, :, lanes(j)]
            grad = jnp.dot(a, left, preferred_element_type=F32) + jnp.dot(
                b, left, preferred_element_type=F32
            )
            grad = grad.astype(BF)
            hg_out[stream, :, lanes(j)] = grad
    first = jnp.full((SCORE_ROW, GROUP_WIDTH), f, jnp.int32) == 0
    row = lax.broadcasted_iota(jnp.int32, (PAD, GROUP_WIDTH), 0)
    for j in range(SLOTS):
        low = jnp.zeros((SCORE_ROW, GROUP_WIDTH), F32)
        high = jnp.zeros((SCORE_ROW, GROUP_WIDTH), F32)
        score = jnp.zeros((1, GROUP_WIDTH), F32)
        for stream in range(2):
            tail, value = stream_parts(messages, w1_ref, md_ref, j, stream)
            win = windows_of(tail, value, infos[stream][0])
            grad = hg_out[stream, :, lanes(j)]
            dims = (((0,), (0,)), ((), ()))
            low = low + lax.dot_general(
                jnp.concatenate(win[:2], axis=1), grad, dims, preferred_element_type=F32
            )
            high = high + lax.dot_general(
                jnp.concatenate(win[2:], axis=1), grad, dims, preferred_element_type=F32
            )
            score = score + jnp.sum(
                columns[stream] * h_ref[stream, :, lanes(j)], axis=0, keepdims=True
            )
        base = j * (SCORE_ROW + PAD)
        score = jnp.where(row == 0, jnp.broadcast_to(score, row.shape), 0.0)
        mine_out[base : base + SCORE_ROW, :] = jnp.where(first, low, high)
        send_out[base : base + SCORE_ROW, :] = jnp.where(first, high, low)
        mine_out[base + SCORE_ROW : base + SCORE_ROW + PAD, :] = score
        send_out[base + SCORE_ROW : base + SCORE_ROW + PAD, :] = score


def add_kernel(mine_ref, got_ref, edge_ref, *outs):
    for j, out in zip(range(1, SLOTS), outs):
        base = j * (SCORE_ROW + PAD)
        total = mine_ref[base : base + SCORE_ROW + PAD, :] + got_ref[base : base + SCORE_ROW + PAD, :]
        out[0:SCORE_ROW, :] = total[0:SCORE_ROW].astype(BF)
        a, b = two_terms(total[SCORE_ROW:])
        out[SCORE_ROW:HALO_ROW, :] = jnp.concatenate([a.astype(F32), b.astype(F32)], axis=0).astype(BF)
        if j == 1:
            for slot in range(SLOTS):
                edge = edge_ref[:, lanes(slot)]
                out[HALO_ROW + PAD * slot : HALO_ROW + PAD * (slot + 1), :] = edge


def sum_kernel(mine_ref, got_ref, z1, z2, z3, out_ref, score_ref):
    f = lax.axis_index("fsdp")
    total = mine_ref[0 : SCORE_ROW + PAD, :] + got_ref[0 : SCORE_ROW + PAD, :]
    grad, score = total[0:SCORE_ROW], total[SCORE_ROW:]
    for ref in (z1, z2, z3):
        grad = grad + ref[0:SCORE_ROW, :].astype(F32)
        pair = ref[SCORE_ROW:HALO_ROW, :].astype(F32)
        score = score + pair[0:PAD] + pair[PAD:]
    out_ref[...] = grad
    half = GROUP_WIDTH // 2
    score_ref[...] = jnp.where(
        jnp.full((1, half), f, jnp.int32) == 0, score[0:1, :half], score[0:1, half:]
    )


def input_kernel(files, hg_ref, mine_ref, other_ref, *refs):
    w_refs, outs = refs[: 2 * SLOTS], refs[2 * SLOTS :]
    rows = hg_ref.shape[1]
    halves = [kernel_halves(w_refs, j) for j in range(SLOTS)]
    for stream, message in enumerate((mine_ref, other_ref)):
        since, _ = row_info(message, files)
        for j in range(SLOTS):
            grad = hg_ref[stream, :, lanes(j)].astype(F32)
            total = jnp.zeros((PAD + rows, GROUP_WIDTH), F32)
            for lag in range(KERNEL):
                kept = grad if lag == 0 else jnp.where(since >= lag, grad, 0.0)
                window = jnp.concatenate([jnp.zeros((PAD, GROUP_WIDTH), F32), kept], axis=0)
                if lag > 0:
                    window = pltpu.roll(window, PAD + rows - lag, 0)
                part = halves[j][lag // 2][GROUP_WIDTH * (lag % 2) : GROUP_WIDTH * (lag % 2 + 1)]
                total = total + nt(window.astype(BF), part)
            outs[stream][:, lanes(j)] = total[PAD:].astype(BF)
            outs[2 + stream][:, lanes((j + SLOTS - 1) % SLOTS)] = total[0:PAD].astype(BF)


def place_kernel(own_ref, got_ref, z1_ref, edge_ref, out_ref):
    rows = own_ref.shape[0]
    s, d = lax.axis_index("seq"), lax.axis_index("dp")
    inside = jnp.full((2 * PAD, GROUP_WIDTH), s, jnp.int32) < SLOTS - 1
    none = jnp.zeros((PAD, GROUP_WIDTH), F32)
    for j in range(SLOTS):
        own_edge = z1_ref[HALO_ROW + PAD * j : HALO_ROW + PAD * (j + 1), :]
        for ref, edge, parity in ((own_ref, own_edge, d), (got_ref, edge_ref[:, lanes(j)], 1 - d)):
            col = group_lanes(slot_group(s, j, parity))
            out_ref[0, 0 : rows - 2 * PAD, col] = ref[0 : rows - 2 * PAD, lanes(j)]
            extra = jnp.where(inside, jnp.concatenate([none, edge.astype(F32)], axis=0), 0.0)
            last = ref[rows - 2 * PAD :, lanes(j)].astype(F32) + extra
            out_ref[0, rows - 2 * PAD :, col] = last.astype(BF)


def per_device_paired(inputs, conv_weight, score_weight, lengths, offsets, cotangent):
    rows, pairs, files = inputs.shape[1], cotangent.shape[1], offsets.shape[1]
    shape = jax.ShapeDtypeStruct

    def flip(value, axis):
        return lax.ppermute(value, axis, [(0, 1), (1, 0)])

    def cycle(value, by):
        return lax.ppermute(value, "seq", [(i, (i + by) % SLOTS) for i in range(SLOTS)])

    def across(value, by):
        pairs_of = [
            (i * 2 + j, (i + by) * 2 + 1 - j)
            for i in range(SLOTS)
            for j in range(2)
            if 0 <= i + by < SLOTS
        ]
        return lax.ppermute(value, ("seq", "dp"), pairs_of)

    wide = HALO_ROW + PAD * SLOTS
    message = shape((rows + pairs + PAD, HALF), BF)
    mine, other, mw, mw1, md = call(
        pack_kernel,
        (
            message,
            message,
            shape((HALO_ROW, GROUP_WIDTH), BF),
            shape((wide, GROUP_WIDTH), BF),
            shape((PAD, HALF), BF),
        ),
        scratch=(
            pltpu.SMEM(offsets.shape, jnp.int32),
            pltpu.VMEM(inputs.shape, BF),
            pltpu.VMEM(cotangent.shape, BF),
            pltpu.VMEM((1, score_weight.shape[0]), BF),
            pltpu.SemaphoreType.DMA((6,)),
        ),
        hbm=5,
    )(*(pltpu.with_memory_space_constraint(v, pltpu.HBM) for v in (offsets, inputs, cotangent, conv_weight, score_weight.reshape(1, -1))), lengths.reshape(1, 1))
    other = flip(other, "dp")
    shards = [mw, cycle(mw1, 1), cycle(mw, 2), cycle(mw, 3)]
    mdr = across(md, 1)
    shards = shards + [flip(w, "fsdp") for w in shards]
    hidden, left, partial = call(
        functools.partial(hidden_kernel, files),
        (
            shape((2, rows, HALF), F32),
            shape((2, pairs + PAD, HALF), BF),
            shape((2, 16, GROUP_WIDTH), F32),
        ),
    )(mine, other, mdr, *shards)
    partial_r = flip(partial, "dp")
    grad_rows = SLOTS * (SCORE_ROW + PAD)
    hg, kept, send = call(
        functools.partial(mix_kernel, files),
        (
            shape((2, rows, HALF), BF),
            shape((grad_rows, GROUP_WIDTH), F32),
            shape((grad_rows, GROUP_WIDTH), F32),
        ),
    )(mine, other, mdr, shards[1], hidden, left, partial, partial_r)
    got = flip(send, "fsdp")
    x_own, x_send, edge_own, edge_send = call(
        functools.partial(input_kernel, files),
        (
            shape((rows, HALF), BF),
            shape((rows, HALF), BF),
            shape((PAD, HALF), BF),
            shape((PAD, HALF), BF),
        ),
    )(hg, mine, other, *shards)
    x_got = flip(x_send, "dp")
    edge_got = across(edge_send, -1)
    sums = call(
        add_kernel,
        (
            shape((wide, GROUP_WIDTH), BF),
            shape((HALO_ROW, GROUP_WIDTH), BF),
            shape((HALO_ROW, GROUP_WIDTH), BF),
        ),
    )(kept, got, edge_own)
    final = [cycle(value, -j) for j, value in zip(range(1, SLOTS), sums)]
    input_grad = call(place_kernel, shape(inputs.shape, BF))(x_own, x_got, final[0], edge_got)
    kernel_grad, score_grad = call(
        sum_kernel,
        (shape((SCORE_ROW, GROUP_WIDTH), F32), shape((1, GROUP_WIDTH // 2), F32)),
    )(kept, got, *final)
    return (input_grad, kernel_grad, score_grad.reshape(-1))


def solution(mesh):
    placed = (
        P(("parts", "dp", "fsdp"), "seq", None),
        P(("seq", "dp", "fsdp"), None),
        P(("seq", "dp", "fsdp")),
        P(("parts", "dp", "fsdp")),
        P(("parts", "dp", "fsdp"), None),
        P(("parts", "dp", "fsdp"), "seq", None),
    )
    paired = mesh.shape["seq"] == SLOTS and mesh.shape["dp"] == 2 and mesh.shape["fsdp"] == 2
    return jax.shard_map(
        per_device_paired if paired else per_device_general,
        mesh=mesh,
        in_specs=placed,
        out_specs=(
            P(("parts", "dp", "fsdp"), "seq", None),
            P(("parts", "seq", "dp", "fsdp"), None),
            P(("parts", "seq", "dp", "fsdp")),
        ),
        check_vma=False,
    )
```

```python
import functools

import jax
import jax.numpy as jnp
from jax import lax
from jax.experimental import pallas as pl
from jax.experimental.pallas import tpu as pltpu
from jax.sharding import PartitionSpec as P

GROUPS = 8
KERNEL = 4
GROUP_WIDTH = 128


precise_mode = lax.Precision.HIGHEST


def shifted(value, axis, by):
    devices = lax.axis_size(axis)
    pairs = [(i, i + by) for i in range(devices) if 0 <= i + by < devices]
    return lax.ppermute(value, axis, pairs)


def segment_of(positions, offsets):
    return jnp.sum((offsets[None, :] <= positions[:, None]).astype(jnp.int32), axis=1)


def tap_valid(positions, offsets, lag_steps):
    earlier = positions - lag_steps
    same_file = segment_of(positions, offsets) == segment_of(earlier, offsets)
    return jnp.logical_and(earlier >= 0, same_file)


def mix_backward(hidden, upstream, score_vec):
    row_count = hidden.shape[0]
    width_all = hidden.shape[1]
    pooled_list = []
    logit_list = []
    for block_size in range(1, 5):
        pooled = hidden.reshape(row_count // block_size, block_size, width_all).sum(axis=1) * (
            1.0 / block_size
        )
        pooled_list.append(pooled)
        logit_list.append(
            jnp.repeat(jnp.dot(pooled, score_vec, precision=precise_mode), block_size)
        )
    logits = jnp.stack(logit_list)
    exp_logits = jnp.exp(logits)
    choose_prob = exp_logits / jnp.sum(exp_logits, axis=0)
    mix_grad = jnp.repeat(upstream.astype(jnp.float32) * 0.5, 2, axis=0)
    inner_list = []
    for block_size in range(1, 5):
        pooled = pooled_list[block_size - 1]
        inner = jnp.sum(
            mix_grad.reshape(row_count // block_size, block_size, width_all) * pooled[:, None, :],
            axis=2,
        )
        inner_list.append(inner.reshape(row_count))
    inner_all = jnp.stack(inner_list)
    dlogit = choose_prob * (inner_all - jnp.sum(choose_prob * inner_all, axis=0))
    hidden_grad = jnp.zeros((row_count, width_all), jnp.float32)
    weight_grad = jnp.zeros((width_all,), jnp.float32)
    for block_size in range(1, 5):
        block_logit = (
            dlogit[block_size - 1].reshape(row_count // block_size, block_size).sum(axis=1)
        )
        block_mix = (
            (choose_prob[block_size - 1][:, None] * mix_grad)
            .reshape(row_count // block_size, block_size, width_all)
            .sum(axis=1)
        )
        block_term = (block_mix + block_logit[:, None] * score_vec[None, :]) * (1.0 / block_size)
        hidden_grad = hidden_grad + jnp.repeat(block_term, block_size, axis=0)
        weight_grad = weight_grad + jnp.dot(
            block_logit, pooled_list[block_size - 1], precision=precise_mode
        )
    return (hidden_grad, weight_grad)


def per_device_general(inputs, conv_weight, score_weight, lengths, offsets, cotangent):
    local_rows = inputs.shape[1]
    width_all = inputs.shape[2]
    kernel_flat, score_full = (
        lax.all_gather(conv_weight, ("seq", "dp", "fsdp"), axis=0, tiled=True),
        lax.all_gather(score_weight, ("seq", "dp", "fsdp"), axis=0, tiled=True),
    )
    kernel_full = kernel_flat.reshape(GROUPS, KERNEL, GROUP_WIDTH, GROUP_WIDTH)
    score_vec = score_full.astype(jnp.float32)
    start_row = lax.axis_index("seq") * local_rows
    positions = start_row + jnp.arange(local_rows, dtype=jnp.int32)
    own_rows = inputs[0]
    file_starts = offsets[0]
    valid = (positions < lengths[0]).astype(jnp.float32)
    left_rows = shifted(own_rows[local_rows - (KERNEL - 1) :], "seq", 1)
    padded = jnp.concatenate([left_rows, own_rows], axis=0)
    windows = []
    hidden = jnp.zeros((local_rows, GROUPS, GROUP_WIDTH), jnp.float32)
    for tap_index in range(KERNEL):
        window = padded[KERNEL - 1 - tap_index : KERNEL - 1 - tap_index + local_rows]
        keep = tap_valid(positions, file_starts, tap_index)
        window = jnp.where(keep[:, None], window, jnp.zeros_like(window)).reshape(
            local_rows, GROUPS, GROUP_WIDTH
        )
        windows.append(window)
        hidden = hidden + jnp.einsum(
            "ngc,gco->ngo", window, kernel_full[:, tap_index], preferred_element_type=jnp.float32
        )
    hidden = hidden.reshape(local_rows, width_all) * valid[:, None]
    hidden_grad, weight_grad = mix_backward(hidden, cotangent[0], score_vec)
    hidden_low = (hidden_grad * valid[:, None]).astype(jnp.bfloat16)
    right_rows = shifted(hidden_low[: KERNEL - 1], "seq", -1)
    grad_padded = jnp.concatenate([hidden_low, right_rows], axis=0)
    hidden_groups = hidden_low.reshape(local_rows, GROUPS, GROUP_WIDTH)
    input_grad = jnp.zeros((local_rows, GROUPS, GROUP_WIDTH), jnp.float32)
    kernel_terms = []
    for tap_index in range(KERNEL):
        window = grad_padded[tap_index : tap_index + local_rows]
        keep = tap_valid(positions + tap_index, file_starts, tap_index)
        window = jnp.where(keep[:, None], window, jnp.zeros_like(window)).reshape(
            local_rows, GROUPS, GROUP_WIDTH
        )
        input_grad = input_grad + jnp.einsum(
            "ngo,gco->ngc", window, kernel_full[:, tap_index], preferred_element_type=jnp.float32
        )
        kernel_terms.append(
            jnp.einsum(
                "ngc,ngo->gco",
                windows[tap_index],
                hidden_groups,
                preferred_element_type=jnp.float32,
            )
        )
    input_grad = input_grad.reshape(local_rows, width_all).astype(jnp.bfloat16)[None]
    kernel_part = jnp.stack(kernel_terms, axis=1).reshape(
        GROUPS * KERNEL * GROUP_WIDTH, GROUP_WIDTH
    )
    kernel_grad, score_grad = (
        lax.psum_scatter(kernel_part, ("seq", "dp", "fsdp"), scatter_dimension=0, tiled=True),
        lax.psum_scatter(weight_grad, ("seq", "dp", "fsdp"), scatter_dimension=0, tiled=True),
    )
    return (input_grad, kernel_grad, score_grad)


SLOTS = 4
HALF = SLOTS * GROUP_WIDTH
PAD = 8
SCORE_ROW = 2 * GROUP_WIDTH
HALO_ROW = SCORE_ROW + 16
SHARD = HALO_ROW
AHEAD = 4
HEAD = 6
BF = jnp.bfloat16
F32 = jnp.float32


def lanes(slot):
    return slice(slot * GROUP_WIDTH, (slot + 1) * GROUP_WIDTH)


def group_lanes(group):
    return pl.ds(pl.multiple_of(group * GROUP_WIDTH, GROUP_WIDTH), GROUP_WIDTH)


def slot_group(seq, slot, parity):
    return 2 * lax.rem(seq - slot + 2 * SLOTS, SLOTS) + parity


def call(body, out_shape, scratch=(), hbm=0, cost=None):
    def run(*args):
        specs = [pl.BlockSpec(memory_space=pltpu.HBM)] * hbm
        specs += [pl.BlockSpec(memory_space=pltpu.VMEM)] * (len(args) - hbm)
        return pl.pallas_call(
            body,
            out_shape=out_shape,
            in_specs=specs,
            out_specs=jax.tree.map(lambda _: pl.BlockSpec(memory_space=pltpu.VMEM), out_shape),
            scratch_shapes=list(scratch),
            cost_estimate=cost,
            compiler_params=pltpu.CompilerParams(vmem_limit_bytes=48 * 1024 * 1024),
        )(*args)

    return run


def appended(half, slot):
    first = HALO_ROW + PAD * (SLOTS * half + slot)
    return slice(first, first + PAD)


def pack_kernel(off_hbm, x_hbm, c_hbm, w_hbm, score_hbm, len_ref, mine, other, mw1, mw2, mw3,
                off_ref, x_ref, c_ref, score_ref, sems):
    rows, pairs, files = x_ref.shape[1], c_ref.shape[1], off_ref.shape[1]
    s, d, f = (lax.axis_index(name) for name in ("seq", "dp", "fsdp"))
    copies = [
        pltpu.make_async_copy(source, target, sems.at[i])
        for i, (source, target) in enumerate(
            (
                (x_hbm, x_ref),
                (c_hbm, c_ref),
                (off_hbm, off_ref),
                (score_hbm, score_ref),
                (w_hbm, mw1.at[0:SCORE_ROW]),
                (w_hbm, mw2.at[0:SCORE_ROW]),
                (w_hbm, mw3.at[0:SCORE_ROW]),
            )
        )
    ]
    for copy in copies:
        copy.start()
    for copy in copies[2:4]:
        copy.wait()
    lane = lax.broadcasted_iota(jnp.int32, (PAD, GROUP_WIDTH), 1)
    tile_row = lax.broadcasted_iota(jnp.int32, (PAD, GROUP_WIDTH), 0)
    start = s * rows
    info = jnp.zeros((PAD, GROUP_WIDTH), jnp.int32)
    for i in range(files):
        info = jnp.where(lane == i, jnp.clip(off_ref[0, i] - start, -4, rows + PAD), info)
    info = jnp.where(lane == files, jnp.clip(len_ref[0:1, 0:1] - start, 0, rows + PAD), info)
    info = (info.astype(F32) * 0.25).astype(BF)
    value = score_ref[...].astype(F32)
    both = jnp.concatenate([value, value], axis=1)
    half = lax.broadcasted_iota(jnp.int32, (16, GROUP_WIDTH), 1) // (GROUP_WIDTH // 2)
    row = lax.broadcasted_iota(jnp.int32, (16, GROUP_WIDTH), 0)
    block = jnp.where((half == f) & (row == 0), jnp.broadcast_to(both, (16, GROUP_WIDTH)), 0.0)
    for ref in (mw1, mw2, mw3):
        ref[SCORE_ROW:HALO_ROW, :] = block.astype(BF)
    copies[0].wait()
    for ref, parity in ((other, 1 - d), (mine, d)):
        for j in range(SLOTS):
            ref[0:rows, lanes(j)] = x_ref[0, :, group_lanes(slot_group(s, j, parity))]
    for half, parity in ((0, d), (1, 1 - d)):
        for j in range(SLOTS):
            after = group_lanes(slot_group(s + 1, j, parity))
            mw1[appended(half, j), :] = x_ref[0, rows - PAD :, after]
    copies[1].wait()
    for ref, parity in ((other, 1 - d), (mine, d)):
        for j in range(SLOTS):
            col = group_lanes(slot_group(s, j, parity))
            ref[rows : rows + pairs, lanes(j)] = c_ref[0, :, col]
        ref[rows + pairs :, :] = jnp.zeros((PAD, HALF), BF)
        ref[rows + pairs :, lanes(0)] = info
    for half, parity in ((0, d), (1, 1 - d)):
        for j in range(SLOTS):
            before = group_lanes(slot_group(s - 1, j, parity))
            moved = pltpu.roll(c_ref[0, 0:PAD, before].astype(F32), HEAD, 0)
            head = jnp.where(tile_row < HEAD, x_ref[0, 0:PAD, before].astype(F32), moved)
            mw3[appended(half, j), :] = head.astype(BF)
    for copy in copies[4:]:
        copy.wait()


def join_kernel(w0, w1, w2, w3, joined, halo_own, halo_flip):
    for j, ref in enumerate((w0, w1, w2, w3)):
        joined[SHARD * j : SHARD * (j + 1), :] = ref[0:SHARD, :]
    for half, out in enumerate((halo_own, halo_flip)):
        for j in range(SLOTS):
            out[0:PAD, lanes(j)] = w1[appended(half, j), :]
            out[PAD:, lanes(j)] = w3[appended(half, j), :]


def row_info(message, files, first, count):
    info = message[message.shape[0] - PAD :, lanes(0)].astype(F32)[0:1] * 4.0
    lane = lax.broadcasted_iota(jnp.int32, (1, GROUP_WIDTH), 1)
    length = jnp.sum(jnp.where(lane == files, info, 0.0), axis=1, keepdims=True)
    pos = lax.broadcasted_iota(jnp.int32, (count, GROUP_WIDTH), 0).astype(F32) + first
    starts = jnp.where((lane < files) & (info <= pos), info, -4096.0)
    since = pos - jnp.max(starts, axis=1, keepdims=True)
    return since, (pos < length).astype(F32)


def block_weights(count, ahead=0, start=0):
    q = lax.broadcasted_iota(jnp.int32, (count, GROUP_WIDTH), 0)
    r = lax.broadcasted_iota(jnp.int32, (count, GROUP_WIDTH), 1)
    if ahead:
        q = jnp.where(q < start, q, q + (ahead - start))

    def over(value, size):
        if size == 1:
            return value
        if size == 3:
            return lax.shift_right_logical(value * 21846, 16)
        return lax.shift_right_logical(value, size // 2)

    return [
        [
            jnp.where(over(q, size) == over(2 * r + odd, size), 1.0 / size, 0.0).astype(F32)
            for size in range(1, 5)
        ]
        for odd in range(2)
    ]


def message_rows(message):
    return (message.shape[0] - PAD) // 3 * 2


def windows_of(message, tail, j, since):
    value = message[0 : message_rows(message), lanes(j)]
    padded = jnp.concatenate([tail.astype(F32), value.astype(F32)], axis=0)
    out = [value]
    for lag in range(1, KERNEL):
        moved = pltpu.roll(padded, lag, 0)[PAD:]
        out.append(jnp.where(since >= lag, moved, 0.0).astype(BF))
    return out


def edge_windows_of(message, halo_ref, j, since):
    rows = message_rows(message)
    none = jnp.zeros((PAD, GROUP_WIDTH), F32)
    halo = halo_ref[:, lanes(j)].astype(F32)
    last = message[rows - 2 * PAD : rows, lanes(j)].astype(F32)[PAD:]
    before = jnp.concatenate([halo[:PAD], none], axis=0)
    after = jnp.concatenate([last, halo[PAD:]], axis=0)
    out = []
    for lag in range(KERNEL):
        shift = [pltpu.roll(v, lag, 0)[PAD:] if lag else v[PAD:] for v in (before, after)]
        moved = jnp.concatenate(shift, axis=0)
        out.append(jnp.where(since >= lag, moved, 0.0).astype(BF))
    return out


def kernel_rows(w_refs, j):
    return jnp.concatenate(kernel_halves(w_refs, j), axis=0)


def kernel_halves(w_refs, j):
    f = lax.axis_index("fsdp")
    mine, theirs = (ref[SHARD * j : SHARD * j + SCORE_ROW, :] for ref in w_refs)
    first = jnp.full((SCORE_ROW, GROUP_WIDTH), f, jnp.int32) == 0
    return jnp.where(first, mine, theirs), jnp.where(first, theirs, mine)


def nt(a, b):
    return lax.dot_general(a, b, (((1,), (1,)), ((), ())), preferred_element_type=F32)


def two_terms(value):
    high = value.astype(BF)
    return high, (value - high.astype(F32)).astype(BF)


def gram_of(hidden, left):
    a, b = two_terms(hidden)
    return nt(a, left) + nt(b, left)


def block_sums(weights, gram, column):
    inner = [
        jnp.sum(weights[odd][b] * gram, axis=0, keepdims=True) * 0.5
        for odd in range(2)
        for b in range(4)
    ]
    logit = [
        jnp.sum(weights[odd][b] * column, axis=0, keepdims=True)
        for odd in range(2)
        for b in range(4)
    ]
    return jnp.concatenate(inner + logit, axis=0)


def hidden_kernel(files, mine_ref, other_ref, wm_ref, wt_ref, h_out, l_out, r_out):
    messages = (mine_ref, other_ref)
    rows = h_out.shape[1]
    pairs = rows // 2
    infos = [row_info(ref, files, 0, rows) for ref in messages]
    row = lax.broadcasted_iota(jnp.int32, (PAD, GROUP_WIDTH), 0)
    none = jnp.zeros((PAD, GROUP_WIDTH), F32)
    for j in range(SLOTS):
        kernel = kernel_rows((wm_ref, wt_ref), j)
        score_rows = slice(SHARD * j + SCORE_ROW, SHARD * (j + 1))
        score = wm_ref[score_rows, :].astype(F32) + wt_ref[score_rows, :].astype(F32)
        score = jnp.where(row == AHEAD, jnp.broadcast_to(score[0:1], row.shape), 0.0)
        for stream in range(2):
            since, valid = infos[stream]
            win = jnp.concatenate(windows_of(messages[stream], none, j, since), axis=1)
            hidden = jnp.dot(win, kernel, preferred_element_type=F32)
            h_out[stream, :, lanes(j)] = hidden * valid
            cot = messages[stream][rows : rows + pairs, lanes(j)]
            left = jnp.concatenate([cot.astype(F32), score], axis=0).astype(BF)
            l_out[stream, :, lanes(j)] = left
    weights = block_weights(rows)
    scored = pairs + AHEAD
    for stream in range(2):
        gram = gram_of(h_out[stream], l_out[stream])
        r_out[stream] = block_sums(weights, gram, gram[:, scored : scored + 1])


def edge_info(message, files):
    rows = message_rows(message)
    first, ahead = row_info(message, files, 0, PAD), row_info(message, files, rows, PAD)
    return [jnp.concatenate(pair, axis=0) for pair in zip(first, ahead)]


def edge_hidden_kernel(files, mine_ref, other_ref, own_halo, other_halo, wm_ref, wt_ref, l_ref,
                       r_ref, h_out, l_out, r_out):
    messages, halos = (mine_ref, other_ref), (own_halo, other_halo)
    rows = message_rows(mine_ref)
    kept = rows // 2 - PAD
    infos = [edge_info(ref, files) for ref in messages]
    row = lax.broadcasted_iota(jnp.int32, (2 * PAD, GROUP_WIDTH), 0)
    for stream in range(2):
        l_out[stream, 0:kept, :] = l_ref[stream, 0:kept, :]
    for j in range(SLOTS):
        kernel = kernel_rows((wm_ref, wt_ref), j)
        wins = [
            jnp.concatenate(edge_windows_of(messages[i], halos[i], j, infos[i][0]), axis=1)
            for i in range(2)
        ]
        hidden = jnp.dot(jnp.concatenate(wins, axis=0), kernel, preferred_element_type=F32)
        for stream in range(2):
            block = hidden[2 * PAD * stream : 2 * PAD * (stream + 1)]
            h_out[stream, :, lanes(j)] = block * infos[stream][1]
            head = halos[stream][:, lanes(j)].astype(F32)
            head = pltpu.roll(head, 2 * PAD - HEAD, 0)
            old = l_ref[stream, kept:, lanes(j)].astype(F32)
            take = (row >= PAD) & (row < PAD + 2)
            l_out[stream, kept:, lanes(j)] = jnp.where(take, head, old).astype(BF)
    weights = block_weights(2 * PAD, rows, PAD)
    scored = rows // 2 + AHEAD
    for stream in range(2):
        gram = gram_of(h_out[stream], l_out[stream])
        column = gram[:, scored : scored + 1]
        r_out[stream] = r_ref[stream] + block_sums(weights, gram, column)


def window_kernel(files, mine_ref, other_ref, own_halo, other_halo, after_ref, out_ref):
    del after_ref
    for stream, (message, halo) in enumerate(((mine_ref, own_halo), (other_ref, other_halo))):
        since, _ = row_info(message, files, 0, message_rows(message))
        for j in range(SLOTS):
            win = windows_of(message, halo[0:PAD, lanes(j)], j, since)
            for lag in range(KERNEL):
                value = jnp.concatenate([win[lag], jnp.zeros((2 * PAD, GROUP_WIDTH), BF)], axis=0)
                span = value.shape[0]
                out_ref[j, lanes(lag), span * stream : span * (stream + 1)] = value.T


def mixing(weights, total, count):
    spread = jnp.zeros((count, GROUP_WIDTH), F32)
    carry = jnp.zeros((count, GROUP_WIDTH), F32)
    for odd in range(2):
        for b in range(4):
            choose, change = total[odd][b]
            spread = spread + weights[odd][b] * choose
            carry = carry + weights[odd][b] * change
    return spread, jnp.sum(carry, axis=1, keepdims=True)


def mix_kernel(files, mine_ref, other_ref, win_ref, h_ref, he_ref, l_ref, r_ref, rr_ref,
               hg_out, hx_out, mine_out, send_out):
    messages = (mine_ref, other_ref)
    rows = h_ref.shape[1]
    scored = rows // 2 + AHEAD
    f = lax.axis_index("fsdp")
    weights = block_weights(rows)
    edge_weights = block_weights(2 * PAD, rows, PAD)
    columns = []
    for stream in range(2):
        summed = r_ref[stream] + rr_ref[1 - stream]
        total = []
        for odd in range(2):
            inner = [summed[4 * odd + b : 4 * odd + b + 1] for b in range(4)]
            logit = [summed[8 + 4 * odd + b : 8 + 4 * odd + b + 1] for b in range(4)]
            top = jnp.maximum(jnp.maximum(logit[0], logit[1]), jnp.maximum(logit[2], logit[3]))
            powers = [jnp.exp(v - top) for v in logit]
            scale = 1.0 / (powers[0] + powers[1] + powers[2] + powers[3])
            choose = [v * scale for v in powers]
            mean = sum(c * m for c, m in zip(choose, inner))
            total.append([(c * 0.5, c * (m - mean)) for c, m in zip(choose, inner)])
        parts = (
            (weights, rows, row_info(messages[stream], files, 0, rows)[1]),
            (edge_weights, 2 * PAD, edge_info(messages[stream], files)[1]),
        )
        terms = []
        for part_weights, count, valid in parts:
            spread, e = mixing(part_weights, total, count)
            lane = lax.broadcasted_iota(jnp.int32, (count, GROUP_WIDTH), 1)
            terms.append(two_terms(jnp.where(lane == scored, e, spread) * valid))
            if count == rows:
                columns.append(e)
        left = l_ref[stream]
        grad = jnp.dot(
            jnp.concatenate([jnp.concatenate(pair, axis=1) for pair in terms], axis=0),
            jnp.concatenate([left, left], axis=0),
            preferred_element_type=F32,
        ).astype(BF)
        hg_out[stream] = grad[:rows]
        hx_out[stream] = grad[rows:]
    first = jnp.full((SCORE_ROW, GROUP_WIDTH), f, jnp.int32) == 0
    row = lax.broadcasted_iota(jnp.int32, (PAD, GROUP_WIDTH), 0)
    for j in range(SLOTS):
        none = jnp.zeros((2 * PAD, GROUP_WIDTH), BF)
        grads = [v for i in range(2) for v in (hg_out[i, :, lanes(j)], none)]
        both = jnp.dot(
            win_ref[j], jnp.concatenate(grads, axis=0), preferred_element_type=F32
        )
        low, high = both[:SCORE_ROW], both[SCORE_ROW:]
        score = jnp.zeros((1, GROUP_WIDTH), F32)
        for stream in range(2):
            value = columns[stream] * h_ref[stream, :, lanes(j)]
            edge = columns[stream][0:PAD] * he_ref[stream, 0:PAD, lanes(j)]
            score = score + jnp.sum(value, axis=0, keepdims=True)
            score = score + jnp.sum(edge, axis=0, keepdims=True)
        base = j * (SCORE_ROW + PAD)
        score = jnp.where(row == 0, jnp.broadcast_to(score, row.shape), 0.0)
        mine_out[base : base + SCORE_ROW, :] = jnp.where(first, low, high)
        send_out[base : base + SCORE_ROW, :] = jnp.where(first, high, low)
        mine_out[base + SCORE_ROW : base + SCORE_ROW + PAD, :] = score
        send_out[base + SCORE_ROW : base + SCORE_ROW + PAD, :] = score


def add_kernel(kept_ref, got_ref, *outs):
    for j, out in zip(range(1, SLOTS), outs):
        base = j * (SCORE_ROW + PAD)
        total = kept_ref[base : base + SCORE_ROW + PAD, :] + got_ref[base : base + SCORE_ROW + PAD, :]
        out[0:SCORE_ROW, :] = total[0:SCORE_ROW].astype(BF)
        a, b = two_terms(total[SCORE_ROW:])
        out[SCORE_ROW:, :] = jnp.concatenate([a.astype(F32), b.astype(F32)], axis=0).astype(BF)


def input_half(files, stream, hg_ref, hx_ref, message, w_refs, out):
    rows = hg_ref.shape[1]
    since, _ = row_info(message, files, 0, rows + PAD)
    for j in range(SLOTS):
        halves = kernel_halves(w_refs, j)
        ahead = hx_ref[stream, :, lanes(j)].astype(F32)[PAD:]
        grad = jnp.concatenate([hg_ref[stream, :, lanes(j)].astype(F32), ahead], axis=0)
        total = jnp.zeros((rows + PAD, GROUP_WIDTH), F32)
        for lag in range(KERNEL):
            window = grad if lag == 0 else jnp.where(since >= lag, grad, 0.0)
            if lag > 0:
                window = pltpu.roll(window, rows + PAD - lag, 0)
            part = halves[lag // 2][GROUP_WIDTH * (lag % 2) : GROUP_WIDTH * (lag % 2 + 1)]
            total = total + nt(window.astype(BF), part)
        out[:, lanes(j)] = total[:rows].astype(BF)


def send_kernel(files, hg_ref, hx_ref, other_ref, wm_ref, wt_ref, out):
    input_half(files, 1, hg_ref, hx_ref, other_ref, (wm_ref, wt_ref), out)


def own_kernel(files, hg_ref, hx_ref, mine_ref, wm_ref, wt_ref, x_out, value_ref, sems):
    input_half(files, 0, hg_ref, hx_ref, mine_ref, (wm_ref, wt_ref), value_ref)
    for copy in half_copies(value_ref, x_out, lax.axis_index("dp"), sems):
        copy.wait()


def half_copies(value_ref, x_out, parity, sems):
    s = lax.axis_index("seq")
    copies = [
        pltpu.make_async_copy(
            value_ref.at[:, lanes(j)],
            x_out.at[0, :, group_lanes(slot_group(s, j, parity))],
            sems.at[j],
        )
        for j in range(SLOTS)
    ]
    for copy in copies:
        copy.start()
    return copies


def finish_kernel(kept_ref, got_ref, z1, z2, z3, x_got_ref, x_hbm,
                  x_out, grad_out, score_out, grad_ref, score_ref, sems):
    del x_hbm
    f = lax.axis_index("fsdp")
    copies = half_copies(x_got_ref, x_out, 1 - lax.axis_index("dp"), sems)
    total = kept_ref[0 : SCORE_ROW + PAD, :] + got_ref[0 : SCORE_ROW + PAD, :]
    grad, score = total[0:SCORE_ROW], total[SCORE_ROW:]
    for ref in (z1, z2, z3):
        grad = grad + ref[0:SCORE_ROW, :].astype(F32)
        pair = ref[SCORE_ROW:, :].astype(F32)
        score = score + pair[0:PAD] + pair[PAD:]
    grad_ref[...] = grad
    copy_grad = pltpu.make_async_copy(grad_ref, grad_out, sems.at[SLOTS])
    copy_grad.start()
    half = GROUP_WIDTH // 2
    score_ref[...] = jnp.where(
        jnp.full((1, half), f, jnp.int32) == 0, score[0:1, :half], score[0:1, half:]
    )
    copy_score = pltpu.make_async_copy(score_ref, score_out, sems.at[SLOTS + 1])
    copy_score.start()
    for copy in copies + [copy_grad, copy_score]:
        copy.wait()


def per_device_paired(inputs, conv_weight, score_weight, lengths, offsets, cotangent):
    rows, pairs, files = inputs.shape[1], cotangent.shape[1], offsets.shape[1]
    shape = jax.ShapeDtypeStruct

    def flip(value, axis):
        return lax.ppermute(value, axis, [(0, 1), (1, 0)])

    def cycle(value, by):
        return lax.ppermute(value, "seq", [(i, (i + by) % SLOTS) for i in range(SLOTS)])

    message = shape((rows + pairs + PAD, HALF), BF)
    mine, other, mw1, mw2, mw3 = call(
        pack_kernel,
        (
            message,
            message,
            shape((HALO_ROW + 2 * PAD * SLOTS, GROUP_WIDTH), BF),
            shape((HALO_ROW, GROUP_WIDTH), BF),
            shape((HALO_ROW + 2 * PAD * SLOTS, GROUP_WIDTH), BF),
        ),
        scratch=(
            pltpu.SMEM(offsets.shape, jnp.int32),
            pltpu.VMEM(inputs.shape, BF),
            pltpu.VMEM(cotangent.shape, BF),
            pltpu.VMEM((1, score_weight.shape[0]), BF),
            pltpu.SemaphoreType.DMA((7,)),
        ),
        hbm=5,
    )(*(pltpu.with_memory_space_constraint(v, pltpu.HBM) for v in (offsets, inputs, cotangent, conv_weight, score_weight.reshape(1, -1))), lengths.reshape(1, 1))
    other = flip(other, "dp")
    halo = shape((2 * PAD, HALF), BF)
    kernel_mine, halo_own, halo_other = call(
        join_kernel, (shape((SLOTS * SHARD, GROUP_WIDTH), BF), halo, halo)
    )(mw2, cycle(mw1, 1), cycle(mw2, 2), cycle(mw3, 3))
    halo_other = flip(halo_other, "dp")
    shards = (kernel_mine, flip(kernel_mine, "fsdp"))
    left = shape((2, pairs + PAD, HALF), BF)
    sums = shape((2, 16, GROUP_WIDTH), F32)
    hidden, left_main, partial = call(
        functools.partial(hidden_kernel, files), (shape((2, rows, HALF), F32), left, sums)
    )(mine, other, *shards)
    edge_hidden, left, partial = call(
        functools.partial(edge_hidden_kernel, files),
        (shape((2, 2 * PAD, HALF), F32), left, sums),
    )(mine, other, halo_own, halo_other, *shards, left_main, partial)
    partial_r = flip(partial, "dp")
    windows = call(
        functools.partial(window_kernel, files),
        shape((SLOTS, KERNEL * GROUP_WIDTH, 2 * (rows + 2 * PAD)), BF),
        cost=pl.CostEstimate(flops=0, transcendentals=0, bytes_accessed=2 * 1024 * 1024),
    )(mine, other, halo_own, halo_other, partial)
    grad_rows = SLOTS * (SCORE_ROW + PAD)
    hg, hg_ahead, kept, send = call(
        functools.partial(mix_kernel, files),
        (
            shape((2, rows, HALF), BF),
            shape((2, 2 * PAD, HALF), BF),
            shape((grad_rows, GROUP_WIDTH), F32),
            shape((grad_rows, GROUP_WIDTH), F32),
        ),
    )(mine, other, windows, hidden, edge_hidden, left, partial, partial_r)
    got = flip(send, "fsdp")
    x_send = call(functools.partial(send_kernel, files), shape((rows, HALF), BF))(
        hg, hg_ahead, other, *shards
    )
    x_got = flip(x_send, "dp")
    summed = shape((HALO_ROW, GROUP_WIDTH), BF)
    sums = call(add_kernel, (summed, summed, summed))(kept, got)
    final = [cycle(value, -j) for j, value in zip(range(1, SLOTS), sums)]
    vmem, hbm = pl.BlockSpec(memory_space=pltpu.VMEM), pl.BlockSpec(memory_space=pltpu.HBM)
    params = pltpu.CompilerParams(vmem_limit_bytes=48 * 1024 * 1024)
    input_grad = pl.pallas_call(
        functools.partial(own_kernel, files),
        out_shape=shape(inputs.shape, BF),
        in_specs=[vmem] * 5,
        out_specs=hbm,
        scratch_shapes=[pltpu.VMEM((rows, HALF), BF), pltpu.SemaphoreType.DMA((SLOTS,))],
        compiler_params=params,
        cost_estimate=pl.CostEstimate(flops=0, transcendentals=0, bytes_accessed=4 * 1024 * 1024),
    )(hg, hg_ahead, mine, *shards)
    input_grad, kernel_grad, score_grad = pl.pallas_call(
        finish_kernel,
        out_shape=(
            shape(inputs.shape, BF),
            shape((SCORE_ROW, GROUP_WIDTH), F32),
            shape((1, GROUP_WIDTH // 2), F32),
        ),
        in_specs=[vmem] * 6 + [hbm],
        out_specs=(hbm, hbm, hbm),
        scratch_shapes=[
            pltpu.VMEM((SCORE_ROW, GROUP_WIDTH), F32),
            pltpu.VMEM((1, GROUP_WIDTH // 2), F32),
            pltpu.SemaphoreType.DMA((SLOTS + 2,)),
        ],
        input_output_aliases={6: 0},
        compiler_params=params,
    )(kept, got, *final, x_got, input_grad)
    return (input_grad, kernel_grad, score_grad.reshape(-1))


def solution(mesh):
    placed = (
        P(("parts", "dp", "fsdp"), "seq", None),
        P(("seq", "dp", "fsdp"), None),
        P(("seq", "dp", "fsdp")),
        P(("parts", "dp", "fsdp")),
        P(("parts", "dp", "fsdp"), None),
        P(("parts", "dp", "fsdp"), "seq", None),
    )
    paired = mesh.shape["seq"] == SLOTS and mesh.shape["dp"] == 2 and mesh.shape["fsdp"] == 2
    return jax.shard_map(
        per_device_paired if paired else per_device_general,
        mesh=mesh,
        in_specs=placed,
        out_specs=(
            P(("parts", "dp", "fsdp"), "seq", None),
            P(("parts", "seq", "dp", "fsdp"), None),
            P(("parts", "seq", "dp", "fsdp")),
        ),
        check_vma=False,
    )
```

```python
import functools

import jax
import jax.numpy as jnp
from jax import lax
from jax.experimental import pallas as pl
from jax.experimental.pallas import tpu as pltpu
from jax.sharding import PartitionSpec as P

GROUPS = 8
KERNEL = 4
GROUP_WIDTH = 128


precise_mode = lax.Precision.HIGHEST


def shifted(value, axis, by):
    devices = lax.axis_size(axis)
    pairs = [(i, i + by) for i in range(devices) if 0 <= i + by < devices]
    return lax.ppermute(value, axis, pairs)


def segment_of(positions, offsets):
    return jnp.sum((offsets[None, :] <= positions[:, None]).astype(jnp.int32), axis=1)


def tap_valid(positions, offsets, lag_steps):
    earlier = positions - lag_steps
    same_file = segment_of(positions, offsets) == segment_of(earlier, offsets)
    return jnp.logical_and(earlier >= 0, same_file)


def mix_backward(hidden, upstream, score_vec):
    row_count = hidden.shape[0]
    width_all = hidden.shape[1]
    pooled_list = []
    logit_list = []
    for block_size in range(1, 5):
        pooled = hidden.reshape(row_count // block_size, block_size, width_all).sum(axis=1) * (
            1.0 / block_size
        )
        pooled_list.append(pooled)
        logit_list.append(
            jnp.repeat(jnp.dot(pooled, score_vec, precision=precise_mode), block_size)
        )
    logits = jnp.stack(logit_list)
    exp_logits = jnp.exp(logits)
    choose_prob = exp_logits / jnp.sum(exp_logits, axis=0)
    mix_grad = jnp.repeat(upstream.astype(jnp.float32) * 0.5, 2, axis=0)
    inner_list = []
    for block_size in range(1, 5):
        pooled = pooled_list[block_size - 1]
        inner = jnp.sum(
            mix_grad.reshape(row_count // block_size, block_size, width_all) * pooled[:, None, :],
            axis=2,
        )
        inner_list.append(inner.reshape(row_count))
    inner_all = jnp.stack(inner_list)
    dlogit = choose_prob * (inner_all - jnp.sum(choose_prob * inner_all, axis=0))
    hidden_grad = jnp.zeros((row_count, width_all), jnp.float32)
    weight_grad = jnp.zeros((width_all,), jnp.float32)
    for block_size in range(1, 5):
        block_logit = (
            dlogit[block_size - 1].reshape(row_count // block_size, block_size).sum(axis=1)
        )
        block_mix = (
            (choose_prob[block_size - 1][:, None] * mix_grad)
            .reshape(row_count // block_size, block_size, width_all)
            .sum(axis=1)
        )
        block_term = (block_mix + block_logit[:, None] * score_vec[None, :]) * (1.0 / block_size)
        hidden_grad = hidden_grad + jnp.repeat(block_term, block_size, axis=0)
        weight_grad = weight_grad + jnp.dot(
            block_logit, pooled_list[block_size - 1], precision=precise_mode
        )
    return (hidden_grad, weight_grad)


def per_device_general(inputs, conv_weight, score_weight, lengths, offsets, cotangent):
    local_rows = inputs.shape[1]
    width_all = inputs.shape[2]
    kernel_flat, score_full = (
        lax.all_gather(conv_weight, ("seq", "dp", "fsdp"), axis=0, tiled=True),
        lax.all_gather(score_weight, ("seq", "dp", "fsdp"), axis=0, tiled=True),
    )
    kernel_full = kernel_flat.reshape(GROUPS, KERNEL, GROUP_WIDTH, GROUP_WIDTH)
    score_vec = score_full.astype(jnp.float32)
    start_row = lax.axis_index("seq") * local_rows
    positions = start_row + jnp.arange(local_rows, dtype=jnp.int32)
    own_rows = inputs[0]
    file_starts = offsets[0]
    valid = (positions < lengths[0]).astype(jnp.float32)
    left_rows = shifted(own_rows[local_rows - (KERNEL - 1) :], "seq", 1)
    padded = jnp.concatenate([left_rows, own_rows], axis=0)
    windows = []
    hidden = jnp.zeros((local_rows, GROUPS, GROUP_WIDTH), jnp.float32)
    for tap_index in range(KERNEL):
        window = padded[KERNEL - 1 - tap_index : KERNEL - 1 - tap_index + local_rows]
        keep = tap_valid(positions, file_starts, tap_index)
        window = jnp.where(keep[:, None], window, jnp.zeros_like(window)).reshape(
            local_rows, GROUPS, GROUP_WIDTH
        )
        windows.append(window)
        hidden = hidden + jnp.einsum(
            "ngc,gco->ngo", window, kernel_full[:, tap_index], preferred_element_type=jnp.float32
        )
    hidden = hidden.reshape(local_rows, width_all) * valid[:, None]
    hidden_grad, weight_grad = mix_backward(hidden, cotangent[0], score_vec)
    hidden_low = (hidden_grad * valid[:, None]).astype(jnp.bfloat16)
    right_rows = shifted(hidden_low[: KERNEL - 1], "seq", -1)
    grad_padded = jnp.concatenate([hidden_low, right_rows], axis=0)
    hidden_groups = hidden_low.reshape(local_rows, GROUPS, GROUP_WIDTH)
    input_grad = jnp.zeros((local_rows, GROUPS, GROUP_WIDTH), jnp.float32)
    kernel_terms = []
    for tap_index in range(KERNEL):
        window = grad_padded[tap_index : tap_index + local_rows]
        keep = tap_valid(positions + tap_index, file_starts, tap_index)
        window = jnp.where(keep[:, None], window, jnp.zeros_like(window)).reshape(
            local_rows, GROUPS, GROUP_WIDTH
        )
        input_grad = input_grad + jnp.einsum(
            "ngo,gco->ngc", window, kernel_full[:, tap_index], preferred_element_type=jnp.float32
        )
        kernel_terms.append(
            jnp.einsum(
                "ngc,ngo->gco",
                windows[tap_index],
                hidden_groups,
                preferred_element_type=jnp.float32,
            )
        )
    input_grad = input_grad.reshape(local_rows, width_all).astype(jnp.bfloat16)[None]
    kernel_part = jnp.stack(kernel_terms, axis=1).reshape(
        GROUPS * KERNEL * GROUP_WIDTH, GROUP_WIDTH
    )
    kernel_grad, score_grad = (
        lax.psum_scatter(kernel_part, ("seq", "dp", "fsdp"), scatter_dimension=0, tiled=True),
        lax.psum_scatter(weight_grad, ("seq", "dp", "fsdp"), scatter_dimension=0, tiled=True),
    )
    return (input_grad, kernel_grad, score_grad)


SLOTS = 4
HALF = SLOTS * GROUP_WIDTH
PAD = 8
SCORE_ROW = 2 * GROUP_WIDTH
HALO_ROW = SCORE_ROW + PAD
SHARD = SCORE_ROW + 2 * PAD
AHEAD = 4
HEAD = 6
BF = jnp.bfloat16
F32 = jnp.float32


def lanes(slot):
    return slice(slot * GROUP_WIDTH, (slot + 1) * GROUP_WIDTH)


def group_lanes(group):
    return pl.ds(pl.multiple_of(group * GROUP_WIDTH, GROUP_WIDTH), GROUP_WIDTH)


def slot_group(seq, slot, parity):
    return 2 * lax.rem(seq - slot + 2 * SLOTS, SLOTS) + parity


def call(body, out_shape, scratch=(), hbm=0, cost=None):
    def run(*args):
        specs = [pl.BlockSpec(memory_space=pltpu.HBM)] * hbm
        specs += [pl.BlockSpec(memory_space=pltpu.VMEM)] * (len(args) - hbm)
        return pl.pallas_call(
            body,
            out_shape=out_shape,
            in_specs=specs,
            out_specs=jax.tree.map(lambda _: pl.BlockSpec(memory_space=pltpu.VMEM), out_shape),
            scratch_shapes=list(scratch),
            cost_estimate=cost,
            compiler_params=pltpu.CompilerParams(vmem_limit_bytes=48 * 1024 * 1024),
        )(*args)

    return run


def appended(half, slot):
    first = HALO_ROW + PAD * (SLOTS * half + slot)
    return slice(first, first + PAD)


def pack_kernel(off_hbm, x_hbm, c_hbm, w_hbm, score_hbm, len_ref, mine, other, mw1, mw2, mw3,
                off_ref, x_ref, c_ref, score_ref, sems):
    rows, pairs, files = x_ref.shape[1], c_ref.shape[1], off_ref.shape[1]
    s, d, f = (lax.axis_index(name) for name in ("seq", "dp", "fsdp"))
    copies = [
        pltpu.make_async_copy(source, target, sems.at[i])
        for i, (source, target) in enumerate(
            (
                (x_hbm, x_ref),
                (c_hbm, c_ref),
                (off_hbm, off_ref),
                (score_hbm, score_ref),
                (w_hbm, mw1.at[0:SCORE_ROW]),
                (w_hbm, mw2.at[0:SCORE_ROW]),
                (w_hbm, mw3.at[0:SCORE_ROW]),
            )
        )
    ]
    for copy in copies:
        copy.start()
    for copy in copies[2:4]:
        copy.wait()
    lane = lax.broadcasted_iota(jnp.int32, (PAD, GROUP_WIDTH), 1)
    tile_row = lax.broadcasted_iota(jnp.int32, (PAD, GROUP_WIDTH), 0)
    start = s * rows
    info = jnp.zeros((PAD, GROUP_WIDTH), jnp.int32)
    for i in range(files):
        info = jnp.where(lane == i, jnp.clip(off_ref[0, i] - start, -4, rows + PAD), info)
    info = jnp.where(lane == files, jnp.clip(len_ref[0:1, 0:1] - start, 0, rows + PAD), info)
    info = (info.astype(F32) * 0.25).astype(BF)
    value = score_ref[...].astype(F32)
    both = jnp.concatenate([value, value], axis=1)
    keep = (lane // (GROUP_WIDTH // 2) == f) & (tile_row == 0)
    block = jnp.where(keep, jnp.broadcast_to(both, (PAD, GROUP_WIDTH)), 0.0)
    for ref in (mw1, mw2, mw3):
        ref[SCORE_ROW:HALO_ROW, :] = block.astype(BF)
    copies[0].wait()
    for ref, parity in ((other, 1 - d), (mine, d)):
        for j in range(SLOTS):
            ref[0:rows, lanes(j)] = x_ref[0, :, group_lanes(slot_group(s, j, parity))]
    for half, parity in ((0, d), (1, 1 - d)):
        for j in range(SLOTS):
            after = group_lanes(slot_group(s + 1, j, parity))
            mw1[appended(half, j), :] = x_ref[0, rows - PAD :, after]
    copies[1].wait()
    for ref, parity in ((other, 1 - d), (mine, d)):
        for j in range(SLOTS):
            col = group_lanes(slot_group(s, j, parity))
            ref[rows : rows + pairs, lanes(j)] = c_ref[0, :, col]
        ref[rows + pairs :, :] = jnp.zeros((PAD, HALF), BF)
        ref[rows + pairs :, lanes(0)] = info
    for half, parity in ((0, d), (1, 1 - d)):
        for j in range(SLOTS):
            before = group_lanes(slot_group(s - 1, j, parity))
            moved = pltpu.roll(c_ref[0, 0:PAD, before].astype(F32), HEAD, 0)
            head = jnp.where(tile_row < HEAD, x_ref[0, 0:PAD, before].astype(F32), moved)
            mw3[appended(half, j), :] = head.astype(BF)
    for copy in copies[4:]:
        copy.wait()


def join_kernel(w0, w1, w2, w3, joined, halo_own, halo_flip):
    none = jnp.zeros((SHARD - HALO_ROW, GROUP_WIDTH), F32)
    for j, ref in enumerate((w0, w1, w2, w3)):
        joined[SHARD * j : SHARD * j + SCORE_ROW, :] = ref[0:SCORE_ROW, :]
        score = jnp.concatenate([ref[SCORE_ROW:HALO_ROW, :].astype(F32), none], axis=0)
        joined[SHARD * j + SCORE_ROW : SHARD * (j + 1), :] = score.astype(BF)
    for half, out in enumerate((halo_own, halo_flip)):
        for j in range(SLOTS):
            out[0:PAD, lanes(j)] = w1[appended(half, j), :]
            out[PAD:, lanes(j)] = w3[appended(half, j), :]


def row_info(message, files, first, count):
    info = message[message.shape[0] - PAD :, lanes(0)].astype(F32)[0:1] * 4.0
    lane = lax.broadcasted_iota(jnp.int32, (1, GROUP_WIDTH), 1)
    length = jnp.sum(jnp.where(lane == files, info, 0.0), axis=1, keepdims=True)
    pos = lax.broadcasted_iota(jnp.int32, (count, GROUP_WIDTH), 0).astype(F32) + first
    starts = jnp.where((lane < files) & (info <= pos), info, -4096.0)
    since = pos - jnp.max(starts, axis=1, keepdims=True)
    return since, (pos < length).astype(F32)


def block_weights(count, ahead=0, start=0):
    q = lax.broadcasted_iota(jnp.int32, (count, GROUP_WIDTH), 0)
    r = lax.broadcasted_iota(jnp.int32, (count, GROUP_WIDTH), 1)
    if ahead:
        q = jnp.where(q < start, q, q + (ahead - start))

    def over(value, size):
        if size == 1:
            return value
        if size == 3:
            return lax.shift_right_logical(value * 21846, 16)
        return lax.shift_right_logical(value, size // 2)

    return [
        [
            jnp.where(over(q, size) == over(2 * r + odd, size), 1.0 / size, 0.0).astype(F32)
            for size in range(1, 5)
        ]
        for odd in range(2)
    ]


def message_rows(message):
    return (message.shape[0] - PAD) // 3 * 2


def windows_of(message, tail, j, since):
    value = message[0 : message_rows(message), lanes(j)]
    padded = jnp.concatenate([tail.astype(F32), value.astype(F32)], axis=0)
    out = [value]
    for lag in range(1, KERNEL):
        moved = pltpu.roll(padded, lag, 0)[PAD:]
        out.append(jnp.where(since >= lag, moved, 0.0).astype(BF))
    return out


def edge_windows_of(message, halo_ref, j, since):
    rows = message_rows(message)
    none = jnp.zeros((PAD, GROUP_WIDTH), F32)
    halo = halo_ref[:, lanes(j)].astype(F32)
    last = message[rows - 2 * PAD : rows, lanes(j)].astype(F32)[PAD:]
    before = jnp.concatenate([halo[:PAD], none], axis=0)
    after = jnp.concatenate([last, halo[PAD:]], axis=0)
    out = []
    for lag in range(KERNEL):
        shift = [pltpu.roll(v, lag, 0)[PAD:] if lag else v[PAD:] for v in (before, after)]
        moved = jnp.concatenate(shift, axis=0)
        out.append(jnp.where(since >= lag, moved, 0.0).astype(BF))
    return out


def kernel_rows(w_refs, j):
    return jnp.concatenate(kernel_halves(w_refs, j), axis=0)


def kernel_halves(w_refs, j):
    f = lax.axis_index("fsdp")
    mine, theirs = (ref[SHARD * j : SHARD * j + SCORE_ROW, :] for ref in w_refs)
    first = jnp.full((SCORE_ROW, GROUP_WIDTH), f, jnp.int32) == 0
    return jnp.where(first, mine, theirs), jnp.where(first, theirs, mine)


def nt(a, b):
    return lax.dot_general(a, b, (((1,), (1,)), ((), ())), preferred_element_type=F32)


def two_terms(value):
    high = value.astype(BF)
    return high, (value - high.astype(F32)).astype(BF)


def gram_of(hidden, left):
    a, b = two_terms(hidden)
    return nt(a, left) + nt(b, left)


def block_sums(weights, gram, column):
    inner = [
        jnp.sum(weights[odd][b] * gram, axis=0, keepdims=True) * 0.5
        for odd in range(2)
        for b in range(4)
    ]
    logit = [
        jnp.sum(weights[odd][b] * column, axis=0, keepdims=True)
        for odd in range(2)
        for b in range(4)
    ]
    return jnp.concatenate(inner + logit, axis=0)


def hidden_kernel(files, mine_ref, other_ref, wm_ref, wt_ref, h_out, l_out, r_out):
    messages = (mine_ref, other_ref)
    rows = h_out.shape[1]
    pairs = rows // 2
    infos = [row_info(ref, files, 0, rows) for ref in messages]
    row = lax.broadcasted_iota(jnp.int32, (PAD, GROUP_WIDTH), 0)
    none = jnp.zeros((PAD, GROUP_WIDTH), F32)
    for j in range(SLOTS):
        kernel = kernel_rows((wm_ref, wt_ref), j)
        score_rows = slice(SHARD * j + SCORE_ROW, SHARD * (j + 1))
        score = wm_ref[score_rows, :].astype(F32) + wt_ref[score_rows, :].astype(F32)
        score = jnp.where(row == AHEAD, jnp.broadcast_to(score[0:1], row.shape), 0.0)
        for stream in range(2):
            since, valid = infos[stream]
            win = jnp.concatenate(windows_of(messages[stream], none, j, since), axis=1)
            hidden = jnp.dot(win, kernel, preferred_element_type=F32)
            h_out[stream, :, lanes(j)] = hidden * valid
            cot = messages[stream][rows : rows + pairs, lanes(j)]
            left = jnp.concatenate([cot.astype(F32), score], axis=0).astype(BF)
            l_out[stream, :, lanes(j)] = left
    weights = block_weights(rows)
    scored = pairs + AHEAD
    for stream in range(2):
        gram = gram_of(h_out[stream], l_out[stream])
        r_out[stream] = block_sums(weights, gram, gram[:, scored : scored + 1])


def edge_info(message, files):
    rows = message_rows(message)
    first, ahead = row_info(message, files, 0, PAD), row_info(message, files, rows, PAD)
    return [jnp.concatenate(pair, axis=0) for pair in zip(first, ahead)]


def edge_hidden_kernel(files, mine_ref, other_ref, own_halo, other_halo, wm_ref, wt_ref, l_ref,
                       r_ref, h_out, l_out, r_out):
    messages, halos = (mine_ref, other_ref), (own_halo, other_halo)
    rows = message_rows(mine_ref)
    kept = rows // 2 - PAD
    infos = [edge_info(ref, files) for ref in messages]
    row = lax.broadcasted_iota(jnp.int32, (2 * PAD, GROUP_WIDTH), 0)
    for stream in range(2):
        l_out[stream, 0:kept, :] = l_ref[stream, 0:kept, :]
    for j in range(SLOTS):
        kernel = kernel_rows((wm_ref, wt_ref), j)
        wins = [
            jnp.concatenate(edge_windows_of(messages[i], halos[i], j, infos[i][0]), axis=1)
            for i in range(2)
        ]
        hidden = jnp.dot(jnp.concatenate(wins, axis=0), kernel, preferred_element_type=F32)
        for stream in range(2):
            block = hidden[2 * PAD * stream : 2 * PAD * (stream + 1)]
            h_out[stream, :, lanes(j)] = block * infos[stream][1]
            head = halos[stream][:, lanes(j)].astype(F32)
            head = pltpu.roll(head, 2 * PAD - HEAD, 0)
            old = l_ref[stream, kept:, lanes(j)].astype(F32)
            take = (row >= PAD) & (row < PAD + 2)
            l_out[stream, kept:, lanes(j)] = jnp.where(take, head, old).astype(BF)
    weights = block_weights(2 * PAD, rows, PAD)
    scored = rows // 2 + AHEAD
    for stream in range(2):
        gram = gram_of(h_out[stream], l_out[stream])
        column = gram[:, scored : scored + 1]
        r_out[stream] = r_ref[stream] + block_sums(weights, gram, column)


def window_kernel(files, mine_ref, other_ref, own_halo, other_halo, after_ref, out_ref):
    del after_ref
    for stream, (message, halo) in enumerate(((mine_ref, own_halo), (other_ref, other_halo))):
        since, _ = row_info(message, files, 0, message_rows(message))
        for j in range(SLOTS):
            win = windows_of(message, halo[0:PAD, lanes(j)], j, since)
            for lag in range(KERNEL):
                value = jnp.concatenate([win[lag], jnp.zeros((2 * PAD, GROUP_WIDTH), BF)], axis=0)
                span = value.shape[0]
                out_ref[j, lanes(lag), span * stream : span * (stream + 1)] = value.T


def mixing(weights, total, count):
    spread = jnp.zeros((count, GROUP_WIDTH), F32)
    carry = jnp.zeros((count, GROUP_WIDTH), F32)
    for odd in range(2):
        for b in range(4):
            choose, change = total[odd][b]
            spread = spread + weights[odd][b] * choose
            carry = carry + weights[odd][b] * change
    return spread, jnp.sum(carry, axis=1, keepdims=True)


def mix_kernel(files, mine_ref, other_ref, win_ref, h_ref, he_ref, l_ref, r_ref, rr_ref,
               hg_out, hx_out, mine_out, send_out):
    messages = (mine_ref, other_ref)
    rows = h_ref.shape[1]
    scored = rows // 2 + AHEAD
    f = lax.axis_index("fsdp")
    weights = block_weights(rows)
    edge_weights = block_weights(2 * PAD, rows, PAD)
    columns = []
    for stream in range(2):
        summed = r_ref[stream] + rr_ref[1 - stream]
        total = []
        for odd in range(2):
            inner = [summed[4 * odd + b : 4 * odd + b + 1] for b in range(4)]
            logit = [summed[8 + 4 * odd + b : 8 + 4 * odd + b + 1] for b in range(4)]
            top = jnp.maximum(jnp.maximum(logit[0], logit[1]), jnp.maximum(logit[2], logit[3]))
            powers = [jnp.exp(v - top) for v in logit]
            scale = 1.0 / (powers[0] + powers[1] + powers[2] + powers[3])
            choose = [v * scale for v in powers]
            mean = sum(c * m for c, m in zip(choose, inner))
            total.append([(c * 0.5, c * (m - mean)) for c, m in zip(choose, inner)])
        parts = (
            (weights, rows, row_info(messages[stream], files, 0, rows)[1]),
            (edge_weights, 2 * PAD, edge_info(messages[stream], files)[1]),
        )
        terms = []
        for part_weights, count, valid in parts:
            spread, e = mixing(part_weights, total, count)
            lane = lax.broadcasted_iota(jnp.int32, (count, GROUP_WIDTH), 1)
            terms.append(two_terms(jnp.where(lane == scored, e, spread) * valid))
            if count == rows:
                columns.append(e)
        left = l_ref[stream]
        grad = jnp.dot(
            jnp.concatenate([jnp.concatenate(pair, axis=1) for pair in terms], axis=0),
            jnp.concatenate([left, left], axis=0),
            preferred_element_type=F32,
        ).astype(BF)
        hg_out[stream] = grad[:rows]
        hx_out[stream] = grad[rows:]
    first = jnp.full((SCORE_ROW, GROUP_WIDTH), f, jnp.int32) == 0
    row = lax.broadcasted_iota(jnp.int32, (PAD, GROUP_WIDTH), 0)
    for j in range(SLOTS):
        none = jnp.zeros((2 * PAD, GROUP_WIDTH), BF)
        grads = [v for i in range(2) for v in (hg_out[i, :, lanes(j)], none)]
        both = jnp.dot(
            win_ref[j], jnp.concatenate(grads, axis=0), preferred_element_type=F32
        )
        low, high = both[:SCORE_ROW], both[SCORE_ROW:]
        score = jnp.zeros((1, GROUP_WIDTH), F32)
        for stream in range(2):
            value = columns[stream] * h_ref[stream, :, lanes(j)]
            edge = columns[stream][0:PAD] * he_ref[stream, 0:PAD, lanes(j)]
            score = score + jnp.sum(value, axis=0, keepdims=True)
            score = score + jnp.sum(edge, axis=0, keepdims=True)
        base = j * (SCORE_ROW + PAD)
        score = jnp.where(row == 0, jnp.broadcast_to(score, row.shape), 0.0)
        mine_out[base : base + SCORE_ROW, :] = jnp.where(first, low, high)
        send_out[base : base + SCORE_ROW, :] = jnp.where(first, high, low)
        mine_out[base + SCORE_ROW : base + SCORE_ROW + PAD, :] = score
        send_out[base + SCORE_ROW : base + SCORE_ROW + PAD, :] = score


def add_kernel(kept_ref, got_ref, *outs):
    row = lax.broadcasted_iota(jnp.int32, (PAD, GROUP_WIDTH), 0)
    for j, out in zip(range(1, SLOTS), outs):
        base = j * (SCORE_ROW + PAD)
        total = kept_ref[base : base + SCORE_ROW + PAD, :] + got_ref[base : base + SCORE_ROW + PAD, :]
        out[0:SCORE_ROW, :] = total[0:SCORE_ROW].astype(BF)
        a, b = (jnp.broadcast_to(v.astype(F32)[0:1], row.shape) for v in two_terms(total[SCORE_ROW:]))
        out[SCORE_ROW:, :] = jnp.where(row == 0, a, jnp.where(row == 1, b, 0.0)).astype(BF)


def input_half(files, stream, hg_ref, hx_ref, message, w_refs, out):
    rows = hg_ref.shape[1]
    since, _ = row_info(message, files, 0, rows + PAD)
    for j in range(SLOTS):
        halves = kernel_halves(w_refs, j)
        ahead = hx_ref[stream, :, lanes(j)].astype(F32)[PAD:]
        grad = jnp.concatenate([hg_ref[stream, :, lanes(j)].astype(F32), ahead], axis=0)
        total = jnp.zeros((rows + PAD, GROUP_WIDTH), F32)
        for lag in range(KERNEL):
            window = grad if lag == 0 else jnp.where(since >= lag, grad, 0.0)
            if lag > 0:
                window = pltpu.roll(window, rows + PAD - lag, 0)
            part = halves[lag // 2][GROUP_WIDTH * (lag % 2) : GROUP_WIDTH * (lag % 2 + 1)]
            total = total + nt(window.astype(BF), part)
        out[:, lanes(j)] = total[:rows].astype(BF)


def send_kernel(files, hg_ref, hx_ref, other_ref, wm_ref, wt_ref, out):
    input_half(files, 1, hg_ref, hx_ref, other_ref, (wm_ref, wt_ref), out)


def own_kernel(files, hg_ref, hx_ref, mine_ref, wm_ref, wt_ref, x_out, value_ref, sems):
    input_half(files, 0, hg_ref, hx_ref, mine_ref, (wm_ref, wt_ref), value_ref)
    for copy in half_copies(value_ref, x_out, lax.axis_index("dp"), sems):
        copy.wait()


def half_copies(value_ref, x_out, parity, sems):
    s = lax.axis_index("seq")
    copies = [
        pltpu.make_async_copy(
            value_ref.at[:, lanes(j)],
            x_out.at[0, :, group_lanes(slot_group(s, j, parity))],
            sems.at[j],
        )
        for j in range(SLOTS)
    ]
    for copy in copies:
        copy.start()
    return copies


def finish_kernel(kept_ref, got_ref, z1, z2, z3, x_got_ref, x_hbm,
                  x_out, grad_out, score_out, grad_ref, score_ref, sems):
    del x_hbm
    f = lax.axis_index("fsdp")
    copies = half_copies(x_got_ref, x_out, 1 - lax.axis_index("dp"), sems)
    total = kept_ref[0 : SCORE_ROW + PAD, :] + got_ref[0 : SCORE_ROW + PAD, :]
    grad, score = total[0:SCORE_ROW], total[SCORE_ROW:]
    for ref in (z1, z2, z3):
        grad = grad + ref[0:SCORE_ROW, :].astype(F32)
        pair = ref[SCORE_ROW:, :].astype(F32)
        score = score + jnp.sum(pair, axis=0, keepdims=True)
    grad_ref[...] = grad
    copy_grad = pltpu.make_async_copy(grad_ref, grad_out, sems.at[SLOTS])
    copy_grad.start()
    half = GROUP_WIDTH // 2
    score_ref[...] = jnp.where(
        jnp.full((1, half), f, jnp.int32) == 0, score[0:1, :half], score[0:1, half:]
    )
    copy_score = pltpu.make_async_copy(score_ref, score_out, sems.at[SLOTS + 1])
    copy_score.start()
    for copy in copies + [copy_grad, copy_score]:
        copy.wait()


def per_device_paired(inputs, conv_weight, score_weight, lengths, offsets, cotangent):
    rows, pairs, files = inputs.shape[1], cotangent.shape[1], offsets.shape[1]
    shape = jax.ShapeDtypeStruct

    def flip(value, axis):
        return lax.ppermute(value, axis, [(0, 1), (1, 0)])

    def cycle(value, by):
        return lax.ppermute(value, "seq", [(i, (i + by) % SLOTS) for i in range(SLOTS)])

    message = shape((rows + pairs + PAD, HALF), BF)
    mine, other, mw1, mw2, mw3 = call(
        pack_kernel,
        (
            message,
            message,
            shape((HALO_ROW + 2 * PAD * SLOTS, GROUP_WIDTH), BF),
            shape((HALO_ROW, GROUP_WIDTH), BF),
            shape((HALO_ROW + 2 * PAD * SLOTS, GROUP_WIDTH), BF),
        ),
        scratch=(
            pltpu.SMEM(offsets.shape, jnp.int32),
            pltpu.VMEM(inputs.shape, BF),
            pltpu.VMEM(cotangent.shape, BF),
            pltpu.VMEM((1, score_weight.shape[0]), BF),
            pltpu.SemaphoreType.DMA((7,)),
        ),
        hbm=5,
    )(*(pltpu.with_memory_space_constraint(v, pltpu.HBM) for v in (offsets, inputs, cotangent, conv_weight, score_weight.reshape(1, -1))), lengths.reshape(1, 1))
    other = flip(other, "dp")
    halo = shape((2 * PAD, HALF), BF)
    kernel_mine, halo_own, halo_other = call(
        join_kernel, (shape((SLOTS * SHARD, GROUP_WIDTH), BF), halo, halo)
    )(mw2, cycle(mw1, 1), cycle(mw2, 2), cycle(mw3, 3))
    halo_other = flip(halo_other, "dp")
    shards = (kernel_mine, flip(kernel_mine, "fsdp"))
    left = shape((2, pairs + PAD, HALF), BF)
    sums = shape((2, 16, GROUP_WIDTH), F32)
    hidden, left_main, partial = call(
        functools.partial(hidden_kernel, files), (shape((2, rows, HALF), F32), left, sums)
    )(mine, other, *shards)
    edge_hidden, left, partial = call(
        functools.partial(edge_hidden_kernel, files),
        (shape((2, 2 * PAD, HALF), F32), left, sums),
    )(mine, other, halo_own, halo_other, *shards, left_main, partial)
    partial_r = flip(partial, "dp")
    windows = call(
        functools.partial(window_kernel, files),
        shape((SLOTS, KERNEL * GROUP_WIDTH, 2 * (rows + 2 * PAD)), BF),
        cost=pl.CostEstimate(flops=0, transcendentals=0, bytes_accessed=2 * 1024 * 1024),
    )(mine, other, halo_own, halo_other, partial)
    grad_rows = SLOTS * (SCORE_ROW + PAD)
    hg, hg_ahead, kept, send = call(
        functools.partial(mix_kernel, files),
        (
            shape((2, rows, HALF), BF),
            shape((2, 2 * PAD, HALF), BF),
            shape((grad_rows, GROUP_WIDTH), F32),
            shape((grad_rows, GROUP_WIDTH), F32),
        ),
    )(mine, other, windows, hidden, edge_hidden, left, partial, partial_r)
    got = flip(send, "fsdp")
    x_send = call(functools.partial(send_kernel, files), shape((rows, HALF), BF))(
        hg, hg_ahead, other, *shards
    )
    x_got = flip(x_send, "dp")
    summed = shape((HALO_ROW, GROUP_WIDTH), BF)
    sums = call(add_kernel, (summed, summed, summed))(kept, got)
    final = [cycle(value, -j) for j, value in zip(range(1, SLOTS), sums)]
    vmem, hbm = pl.BlockSpec(memory_space=pltpu.VMEM), pl.BlockSpec(memory_space=pltpu.HBM)
    params = pltpu.CompilerParams(vmem_limit_bytes=48 * 1024 * 1024)
    input_grad = pl.pallas_call(
        functools.partial(own_kernel, files),
        out_shape=shape(inputs.shape, BF),
        in_specs=[vmem] * 5,
        out_specs=hbm,
        scratch_shapes=[pltpu.VMEM((rows, HALF), BF), pltpu.SemaphoreType.DMA((SLOTS,))],
        compiler_params=params,
        cost_estimate=pl.CostEstimate(flops=0, transcendentals=0, bytes_accessed=4 * 1024 * 1024),
    )(hg, hg_ahead, mine, *shards)
    input_grad, kernel_grad, score_grad = pl.pallas_call(
        finish_kernel,
        out_shape=(
            shape(inputs.shape, BF),
            shape((SCORE_ROW, GROUP_WIDTH), F32),
            shape((1, GROUP_WIDTH // 2), F32),
        ),
        in_specs=[vmem] * 6 + [hbm],
        out_specs=(hbm, hbm, hbm),
        scratch_shapes=[
            pltpu.VMEM((SCORE_ROW, GROUP_WIDTH), F32),
            pltpu.VMEM((1, GROUP_WIDTH // 2), F32),
            pltpu.SemaphoreType.DMA((SLOTS + 2,)),
        ],
        input_output_aliases={6: 0},
        compiler_params=params,
    )(kept, got, *final, x_got, input_grad)
    return (input_grad, kernel_grad, score_grad.reshape(-1))


def solution(mesh):
    placed = (
        P(("parts", "dp", "fsdp"), "seq", None),
        P(("seq", "dp", "fsdp"), None),
        P(("seq", "dp", "fsdp")),
        P(("parts", "dp", "fsdp")),
        P(("parts", "dp", "fsdp"), None),
        P(("parts", "dp", "fsdp"), "seq", None),
    )
    paired = mesh.shape["seq"] == SLOTS and mesh.shape["dp"] == 2 and mesh.shape["fsdp"] == 2
    return jax.shard_map(
        per_device_paired if paired else per_device_general,
        mesh=mesh,
        in_specs=placed,
        out_specs=(
            P(("parts", "dp", "fsdp"), "seq", None),
            P(("parts", "seq", "dp", "fsdp"), None),
            P(("parts", "seq", "dp", "fsdp")),
        ),
        check_vma=False,
    )
```

```python
import functools

import jax
import jax.numpy as jnp
from jax import lax
from jax.experimental import pallas as pl
from jax.experimental.pallas import tpu as pltpu
from jax.sharding import PartitionSpec as P

GROUPS = 8
KERNEL = 4
GROUP_WIDTH = 128


precise_mode = lax.Precision.HIGHEST


def shifted(value, axis, by):
    devices = lax.axis_size(axis)
    pairs = [(i, i + by) for i in range(devices) if 0 <= i + by < devices]
    return lax.ppermute(value, axis, pairs)


def segment_of(positions, offsets):
    return jnp.sum((offsets[None, :] <= positions[:, None]).astype(jnp.int32), axis=1)


def tap_valid(positions, offsets, lag_steps):
    earlier = positions - lag_steps
    same_file = segment_of(positions, offsets) == segment_of(earlier, offsets)
    return jnp.logical_and(earlier >= 0, same_file)


def mix_backward(hidden, upstream, score_vec):
    row_count = hidden.shape[0]
    width_all = hidden.shape[1]
    pooled_list = []
    logit_list = []
    for block_size in range(1, 5):
        pooled = hidden.reshape(row_count // block_size, block_size, width_all).sum(axis=1) * (
            1.0 / block_size
        )
        pooled_list.append(pooled)
        logit_list.append(
            jnp.repeat(jnp.dot(pooled, score_vec, precision=precise_mode), block_size)
        )
    logits = jnp.stack(logit_list)
    exp_logits = jnp.exp(logits)
    choose_prob = exp_logits / jnp.sum(exp_logits, axis=0)
    mix_grad = jnp.repeat(upstream.astype(jnp.float32) * 0.5, 2, axis=0)
    inner_list = []
    for block_size in range(1, 5):
        pooled = pooled_list[block_size - 1]
        inner = jnp.sum(
            mix_grad.reshape(row_count // block_size, block_size, width_all) * pooled[:, None, :],
            axis=2,
        )
        inner_list.append(inner.reshape(row_count))
    inner_all = jnp.stack(inner_list)
    dlogit = choose_prob * (inner_all - jnp.sum(choose_prob * inner_all, axis=0))
    hidden_grad = jnp.zeros((row_count, width_all), jnp.float32)
    weight_grad = jnp.zeros((width_all,), jnp.float32)
    for block_size in range(1, 5):
        block_logit = (
            dlogit[block_size - 1].reshape(row_count // block_size, block_size).sum(axis=1)
        )
        block_mix = (
            (choose_prob[block_size - 1][:, None] * mix_grad)
            .reshape(row_count // block_size, block_size, width_all)
            .sum(axis=1)
        )
        block_term = (block_mix + block_logit[:, None] * score_vec[None, :]) * (1.0 / block_size)
        hidden_grad = hidden_grad + jnp.repeat(block_term, block_size, axis=0)
        weight_grad = weight_grad + jnp.dot(
            block_logit, pooled_list[block_size - 1], precision=precise_mode
        )
    return (hidden_grad, weight_grad)


def per_device_general(inputs, conv_weight, score_weight, lengths, offsets, cotangent):
    local_rows = inputs.shape[1]
    width_all = inputs.shape[2]
    kernel_flat, score_full = (
        lax.all_gather(conv_weight, ("seq", "dp", "fsdp"), axis=0, tiled=True),
        lax.all_gather(score_weight, ("seq", "dp", "fsdp"), axis=0, tiled=True),
    )
    kernel_full = kernel_flat.reshape(GROUPS, KERNEL, GROUP_WIDTH, GROUP_WIDTH)
    score_vec = score_full.astype(jnp.float32)
    start_row = lax.axis_index("seq") * local_rows
    positions = start_row + jnp.arange(local_rows, dtype=jnp.int32)
    own_rows = inputs[0]
    file_starts = offsets[0]
    valid = (positions < lengths[0]).astype(jnp.float32)
    left_rows = shifted(own_rows[local_rows - (KERNEL - 1) :], "seq", 1)
    padded = jnp.concatenate([left_rows, own_rows], axis=0)
    windows = []
    hidden = jnp.zeros((local_rows, GROUPS, GROUP_WIDTH), jnp.float32)
    for tap_index in range(KERNEL):
        window = padded[KERNEL - 1 - tap_index : KERNEL - 1 - tap_index + local_rows]
        keep = tap_valid(positions, file_starts, tap_index)
        window = jnp.where(keep[:, None], window, jnp.zeros_like(window)).reshape(
            local_rows, GROUPS, GROUP_WIDTH
        )
        windows.append(window)
        hidden = hidden + jnp.einsum(
            "ngc,gco->ngo", window, kernel_full[:, tap_index], preferred_element_type=jnp.float32
        )
    hidden = hidden.reshape(local_rows, width_all) * valid[:, None]
    hidden_grad, weight_grad = mix_backward(hidden, cotangent[0], score_vec)
    hidden_low = (hidden_grad * valid[:, None]).astype(jnp.bfloat16)
    right_rows = shifted(hidden_low[: KERNEL - 1], "seq", -1)
    grad_padded = jnp.concatenate([hidden_low, right_rows], axis=0)
    hidden_groups = hidden_low.reshape(local_rows, GROUPS, GROUP_WIDTH)
    input_grad = jnp.zeros((local_rows, GROUPS, GROUP_WIDTH), jnp.float32)
    kernel_terms = []
    for tap_index in range(KERNEL):
        window = grad_padded[tap_index : tap_index + local_rows]
        keep = tap_valid(positions + tap_index, file_starts, tap_index)
        window = jnp.where(keep[:, None], window, jnp.zeros_like(window)).reshape(
            local_rows, GROUPS, GROUP_WIDTH
        )
        input_grad = input_grad + jnp.einsum(
            "ngo,gco->ngc", window, kernel_full[:, tap_index], preferred_element_type=jnp.float32
        )
        kernel_terms.append(
            jnp.einsum(
                "ngc,ngo->gco",
                windows[tap_index],
                hidden_groups,
                preferred_element_type=jnp.float32,
            )
        )
    input_grad = input_grad.reshape(local_rows, width_all).astype(jnp.bfloat16)[None]
    kernel_part = jnp.stack(kernel_terms, axis=1).reshape(
        GROUPS * KERNEL * GROUP_WIDTH, GROUP_WIDTH
    )
    kernel_grad, score_grad = (
        lax.psum_scatter(kernel_part, ("seq", "dp", "fsdp"), scatter_dimension=0, tiled=True),
        lax.psum_scatter(weight_grad, ("seq", "dp", "fsdp"), scatter_dimension=0, tiled=True),
    )
    return (input_grad, kernel_grad, score_grad)


SLOTS = 4
HALF = SLOTS * GROUP_WIDTH
PAD = 8
SCORE_ROW = 2 * GROUP_WIDTH
HALO_ROW = SCORE_ROW + PAD
SHARD = SCORE_ROW + 2 * PAD
AHEAD = 4
HEAD = 6
SPARE = 16
JOINED_SPARE = 48
BF = jnp.bfloat16
F32 = jnp.float32


def lanes(slot):
    return slice(slot * GROUP_WIDTH, (slot + 1) * GROUP_WIDTH)


def group_lanes(group):
    return pl.ds(pl.multiple_of(group * GROUP_WIDTH, GROUP_WIDTH), GROUP_WIDTH)


def slot_group(seq, slot, parity):
    return 2 * lax.rem(seq - slot + 2 * SLOTS, SLOTS) + parity


def call(body, out_shape, scratch=(), hbm=0, cost=None):
    def run(*args):
        specs = [pl.BlockSpec(memory_space=pltpu.HBM)] * hbm
        specs += [pl.BlockSpec(memory_space=pltpu.VMEM)] * (len(args) - hbm)
        return pl.pallas_call(
            body,
            out_shape=out_shape,
            in_specs=specs,
            out_specs=jax.tree.map(lambda _: pl.BlockSpec(memory_space=pltpu.VMEM), out_shape),
            scratch_shapes=list(scratch),
            cost_estimate=cost,
            compiler_params=pltpu.CompilerParams(vmem_limit_bytes=48 * 1024 * 1024),
        )(*args)

    return run


def appended(half, slot):
    first = HALO_ROW + PAD * (SLOTS * half + slot)
    return slice(first, first + PAD)


def pack_kernel(off_hbm, x_hbm, c_hbm, w_hbm, score_hbm, len_ref, mine, other, mw1, mw2, mw3,
                off_ref, x_ref, c_ref, score_ref, sems):
    rows, pairs, files = x_ref.shape[1], c_ref.shape[1], off_ref.shape[1]
    s, d, f = (lax.axis_index(name) for name in ("seq", "dp", "fsdp"))
    copies = [
        pltpu.make_async_copy(source, target, sems.at[i])
        for i, (source, target) in enumerate(
            (
                (x_hbm, x_ref),
                (c_hbm, c_ref),
                (off_hbm, off_ref),
                (score_hbm, score_ref),
                (w_hbm, mw1.at[0:SCORE_ROW]),
                (w_hbm, mw2.at[0:SCORE_ROW]),
                (w_hbm, mw3.at[0:SCORE_ROW]),
            )
        )
    ]
    for copy in copies:
        copy.start()
    for copy in copies[2:4]:
        copy.wait()
    lane = lax.broadcasted_iota(jnp.int32, (PAD, GROUP_WIDTH), 1)
    tile_row = lax.broadcasted_iota(jnp.int32, (PAD, GROUP_WIDTH), 0)
    start = s * rows
    info = jnp.zeros((PAD, GROUP_WIDTH), jnp.int32)
    for i in range(files):
        info = jnp.where(lane == i, jnp.clip(off_ref[0, i] - start, -4, rows + PAD), info)
    info = jnp.where(lane == files, jnp.clip(len_ref[0:1, 0:1] - start, 0, rows + PAD), info)
    info = (info.astype(F32) * 0.25).astype(BF)
    value = score_ref[...].astype(F32)
    both = jnp.concatenate([value, value], axis=1)
    keep = (lane // (GROUP_WIDTH // 2) == f) & (tile_row == 0)
    block = jnp.where(keep, jnp.broadcast_to(both, (PAD, GROUP_WIDTH)), 0.0)
    for ref in (mw1, mw2, mw3):
        ref[SCORE_ROW:HALO_ROW, :] = block.astype(BF)
    if SPARE:
        mw1[HALO_ROW + 2 * PAD * SLOTS :, :] = jnp.zeros((SPARE, GROUP_WIDTH), BF)
    copies[0].wait()
    for ref, parity in ((other, 1 - d), (mine, d)):
        for j in range(SLOTS):
            ref[0:rows, lanes(j)] = x_ref[0, :, group_lanes(slot_group(s, j, parity))]
    for half, parity in ((0, d), (1, 1 - d)):
        for j in range(SLOTS):
            after = group_lanes(slot_group(s + 1, j, parity))
            mw1[appended(half, j), :] = x_ref[0, rows - PAD :, after]
    copies[1].wait()
    for ref, parity in ((other, 1 - d), (mine, d)):
        for j in range(SLOTS):
            col = group_lanes(slot_group(s, j, parity))
            ref[rows : rows + pairs, lanes(j)] = c_ref[0, :, col]
        ref[rows + pairs :, :] = jnp.zeros((PAD, HALF), BF)
        ref[rows + pairs :, lanes(0)] = info
    for half, parity in ((0, d), (1, 1 - d)):
        for j in range(SLOTS):
            before = group_lanes(slot_group(s - 1, j, parity))
            moved = pltpu.roll(c_ref[0, 0:PAD, before].astype(F32), HEAD, 0)
            head = jnp.where(tile_row < HEAD, x_ref[0, 0:PAD, before].astype(F32), moved)
            mw3[appended(half, j), :] = head.astype(BF)
    for copy in copies[4:]:
        copy.wait()


def join_kernel(w0, w1, w2, w3, joined, halo_own, halo_flip):
    if JOINED_SPARE:
        joined[SLOTS * SHARD :, :] = jnp.zeros((JOINED_SPARE, GROUP_WIDTH), BF)
    none = jnp.zeros((SHARD - HALO_ROW, GROUP_WIDTH), F32)
    for j, ref in enumerate((w0, w1, w2, w3)):
        joined[SHARD * j : SHARD * j + SCORE_ROW, :] = ref[0:SCORE_ROW, :]
        score = jnp.concatenate([ref[SCORE_ROW:HALO_ROW, :].astype(F32), none], axis=0)
        joined[SHARD * j + SCORE_ROW : SHARD * (j + 1), :] = score.astype(BF)
    for half, out in enumerate((halo_own, halo_flip)):
        for j in range(SLOTS):
            out[0:PAD, lanes(j)] = w1[appended(half, j), :]
            out[PAD:, lanes(j)] = w3[appended(half, j), :]


def row_info(message, files, first, count):
    info = message[message.shape[0] - PAD :, lanes(0)].astype(F32)[0:1] * 4.0
    lane = lax.broadcasted_iota(jnp.int32, (1, GROUP_WIDTH), 1)
    length = jnp.sum(jnp.where(lane == files, info, 0.0), axis=1, keepdims=True)
    pos = lax.broadcasted_iota(jnp.int32, (count, GROUP_WIDTH), 0).astype(F32) + first
    starts = jnp.where((lane < files) & (info <= pos), info, -4096.0)
    since = pos - jnp.max(starts, axis=1, keepdims=True)
    return since, (pos < length).astype(F32)


def block_weights(count, ahead=0, start=0):
    q = lax.broadcasted_iota(jnp.int32, (count, GROUP_WIDTH), 0)
    r = lax.broadcasted_iota(jnp.int32, (count, GROUP_WIDTH), 1)
    if ahead:
        q = jnp.where(q < start, q, q + (ahead - start))

    def over(value, size):
        if size == 1:
            return value
        if size == 3:
            return lax.shift_right_logical(value * 21846, 16)
        return lax.shift_right_logical(value, size // 2)

    return [
        [
            jnp.where(over(q, size) == over(2 * r + odd, size), 1.0 / size, 0.0).astype(F32)
            for size in range(1, 5)
        ]
        for odd in range(2)
    ]


def message_rows(message):
    return (message.shape[0] - PAD) // 3 * 2


def windows_of(message, tail, j, since):
    value = message[0 : message_rows(message), lanes(j)]
    padded = jnp.concatenate([tail.astype(F32), value.astype(F32)], axis=0)
    out = [value]
    for lag in range(1, KERNEL):
        moved = pltpu.roll(padded, lag, 0)[PAD:]
        out.append(jnp.where(since >= lag, moved, 0.0).astype(BF))
    return out


def edge_windows_of(message, halo_ref, j, since):
    rows = message_rows(message)
    none = jnp.zeros((PAD, GROUP_WIDTH), F32)
    halo = halo_ref[:, lanes(j)].astype(F32)
    last = message[rows - 2 * PAD : rows, lanes(j)].astype(F32)[PAD:]
    before = jnp.concatenate([halo[:PAD], none], axis=0)
    after = jnp.concatenate([last, halo[PAD:]], axis=0)
    out = []
    for lag in range(KERNEL):
        shift = [pltpu.roll(v, lag, 0)[PAD:] if lag else v[PAD:] for v in (before, after)]
        moved = jnp.concatenate(shift, axis=0)
        out.append(jnp.where(since >= lag, moved, 0.0).astype(BF))
    return out


def kernel_rows(w_refs, j):
    return jnp.concatenate(kernel_halves(w_refs, j), axis=0)


def kernel_halves(w_refs, j):
    f = lax.axis_index("fsdp")
    mine, theirs = (ref[SHARD * j : SHARD * j + SCORE_ROW, :] for ref in w_refs)
    first = jnp.full((SCORE_ROW, GROUP_WIDTH), f, jnp.int32) == 0
    return jnp.where(first, mine, theirs), jnp.where(first, theirs, mine)


def nt(a, b):
    return lax.dot_general(a, b, (((1,), (1,)), ((), ())), preferred_element_type=F32)


def two_terms(value):
    high = value.astype(BF)
    return high, (value - high.astype(F32)).astype(BF)


def gram_of(hidden, left):
    a, b = two_terms(hidden)
    return nt(a, left) + nt(b, left)


def block_sums(weights, gram, column):
    inner = [
        jnp.sum(weights[odd][b] * gram, axis=0, keepdims=True) * 0.5
        for odd in range(2)
        for b in range(4)
    ]
    logit = [
        jnp.sum(weights[odd][b] * column, axis=0, keepdims=True)
        for odd in range(2)
        for b in range(4)
    ]
    return jnp.concatenate(inner + logit, axis=0)


def hidden_kernel(files, mine_ref, other_ref, wm_ref, wt_ref, h_out, l_out, r_out):
    messages = (mine_ref, other_ref)
    rows = h_out.shape[1]
    pairs = rows // 2
    infos = [row_info(ref, files, 0, rows) for ref in messages]
    row = lax.broadcasted_iota(jnp.int32, (PAD, GROUP_WIDTH), 0)
    none = jnp.zeros((PAD, GROUP_WIDTH), F32)
    for j in range(SLOTS):
        kernel = kernel_rows((wm_ref, wt_ref), j)
        score_rows = slice(SHARD * j + SCORE_ROW, SHARD * (j + 1))
        score = wm_ref[score_rows, :].astype(F32) + wt_ref[score_rows, :].astype(F32)
        score = jnp.where(row == AHEAD, jnp.broadcast_to(score[0:1], row.shape), 0.0)
        for stream in range(2):
            since, valid = infos[stream]
            win = jnp.concatenate(windows_of(messages[stream], none, j, since), axis=1)
            hidden = jnp.dot(win, kernel, preferred_element_type=F32)
            h_out[stream, :, lanes(j)] = hidden * valid
            cot = messages[stream][rows : rows + pairs, lanes(j)]
            left = jnp.concatenate([cot.astype(F32), score], axis=0).astype(BF)
            l_out[stream, :, lanes(j)] = left
    weights = block_weights(rows)
    scored = pairs + AHEAD
    for stream in range(2):
        gram = gram_of(h_out[stream], l_out[stream])
        r_out[stream] = block_sums(weights, gram, gram[:, scored : scored + 1])


def edge_info(message, files):
    rows = message_rows(message)
    first, ahead = row_info(message, files, 0, PAD), row_info(message, files, rows, PAD)
    return [jnp.concatenate(pair, axis=0) for pair in zip(first, ahead)]


def edge_hidden_kernel(files, mine_ref, other_ref, own_halo, other_halo, wm_ref, wt_ref, l_ref,
                       r_ref, h_out, l_out, r_out):
    messages, halos = (mine_ref, other_ref), (own_halo, other_halo)
    rows = message_rows(mine_ref)
    kept = rows // 2 - PAD
    infos = [edge_info(ref, files) for ref in messages]
    row = lax.broadcasted_iota(jnp.int32, (2 * PAD, GROUP_WIDTH), 0)
    for stream in range(2):
        l_out[stream, 0:kept, :] = l_ref[stream, 0:kept, :]
    for j in range(SLOTS):
        kernel = kernel_rows((wm_ref, wt_ref), j)
        wins = [
            jnp.concatenate(edge_windows_of(messages[i], halos[i], j, infos[i][0]), axis=1)
            for i in range(2)
        ]
        hidden = jnp.dot(jnp.concatenate(wins, axis=0), kernel, preferred_element_type=F32)
        for stream in range(2):
            block = hidden[2 * PAD * stream : 2 * PAD * (stream + 1)]
            h_out[stream, :, lanes(j)] = block * infos[stream][1]
            head = halos[stream][:, lanes(j)].astype(F32)
            head = pltpu.roll(head, 2 * PAD - HEAD, 0)
            old = l_ref[stream, kept:, lanes(j)].astype(F32)
            take = (row >= PAD) & (row < PAD + 2)
            l_out[stream, kept:, lanes(j)] = jnp.where(take, head, old).astype(BF)
    weights = block_weights(2 * PAD, rows, PAD)
    scored = rows // 2 + AHEAD
    for stream in range(2):
        gram = gram_of(h_out[stream], l_out[stream])
        column = gram[:, scored : scored + 1]
        r_out[stream] = r_ref[stream] + block_sums(weights, gram, column)


def window_kernel(files, mine_ref, other_ref, own_halo, other_halo, after_ref, out_ref):
    del after_ref
    for stream, (message, halo) in enumerate(((mine_ref, own_halo), (other_ref, other_halo))):
        since, _ = row_info(message, files, 0, message_rows(message))
        for j in range(SLOTS):
            win = windows_of(message, halo[0:PAD, lanes(j)], j, since)
            for lag in range(KERNEL):
                value = jnp.concatenate([win[lag], jnp.zeros((2 * PAD, GROUP_WIDTH), BF)], axis=0)
                span = value.shape[0]
                out_ref[j, lanes(lag), span * stream : span * (stream + 1)] = value.T


def mixing(weights, total, count):
    spread = jnp.zeros((count, GROUP_WIDTH), F32)
    carry = jnp.zeros((count, GROUP_WIDTH), F32)
    for odd in range(2):
        for b in range(4):
            choose, change = total[odd][b]
            spread = spread + weights[odd][b] * choose
            carry = carry + weights[odd][b] * change
    return spread, jnp.sum(carry, axis=1, keepdims=True)


def mix_kernel(files, mine_ref, other_ref, win_ref, h_ref, he_ref, l_ref, r_ref, rr_ref,
               hg_out, hx_out, mine_out, send_out):
    messages = (mine_ref, other_ref)
    rows = h_ref.shape[1]
    scored = rows // 2 + AHEAD
    f = lax.axis_index("fsdp")
    weights = block_weights(rows)
    edge_weights = block_weights(2 * PAD, rows, PAD)
    columns = []
    for stream in range(2):
        summed = r_ref[stream] + rr_ref[1 - stream]
        total = []
        for odd in range(2):
            inner = [summed[4 * odd + b : 4 * odd + b + 1] for b in range(4)]
            logit = [summed[8 + 4 * odd + b : 8 + 4 * odd + b + 1] for b in range(4)]
            top = jnp.maximum(jnp.maximum(logit[0], logit[1]), jnp.maximum(logit[2], logit[3]))
            powers = [jnp.exp(v - top) for v in logit]
            scale = 1.0 / (powers[0] + powers[1] + powers[2] + powers[3])
            choose = [v * scale for v in powers]
            mean = sum(c * m for c, m in zip(choose, inner))
            total.append([(c * 0.5, c * (m - mean)) for c, m in zip(choose, inner)])
        parts = (
            (weights, rows, row_info(messages[stream], files, 0, rows)[1]),
            (edge_weights, 2 * PAD, edge_info(messages[stream], files)[1]),
        )
        terms = []
        for part_weights, count, valid in parts:
            spread, e = mixing(part_weights, total, count)
            lane = lax.broadcasted_iota(jnp.int32, (count, GROUP_WIDTH), 1)
            terms.append(two_terms(jnp.where(lane == scored, e, spread) * valid))
            if count == rows:
                columns.append(e)
        left = l_ref[stream]
        grad = jnp.dot(
            jnp.concatenate([jnp.concatenate(pair, axis=1) for pair in terms], axis=0),
            jnp.concatenate([left, left], axis=0),
            preferred_element_type=F32,
        ).astype(BF)
        hg_out[stream] = grad[:rows]
        hx_out[stream] = grad[rows:]
    first = jnp.full((SCORE_ROW, GROUP_WIDTH), f, jnp.int32) == 0
    row = lax.broadcasted_iota(jnp.int32, (PAD, GROUP_WIDTH), 0)
    for j in range(SLOTS):
        none = jnp.zeros((2 * PAD, GROUP_WIDTH), BF)
        grads = [v for i in range(2) for v in (hg_out[i, :, lanes(j)], none)]
        both = jnp.dot(
            win_ref[j], jnp.concatenate(grads, axis=0), preferred_element_type=F32
        )
        low, high = both[:SCORE_ROW], both[SCORE_ROW:]
        score = jnp.zeros((1, GROUP_WIDTH), F32)
        for stream in range(2):
            value = columns[stream] * h_ref[stream, :, lanes(j)]
            edge = columns[stream][0:PAD] * he_ref[stream, 0:PAD, lanes(j)]
            score = score + jnp.sum(value, axis=0, keepdims=True)
            score = score + jnp.sum(edge, axis=0, keepdims=True)
        base = j * (SCORE_ROW + PAD)
        score = jnp.where(row == 0, jnp.broadcast_to(score, row.shape), 0.0)
        mine_out[base : base + SCORE_ROW, :] = jnp.where(first, low, high)
        send_out[base : base + SCORE_ROW, :] = jnp.where(first, high, low)
        mine_out[base + SCORE_ROW : base + SCORE_ROW + PAD, :] = score
        send_out[base + SCORE_ROW : base + SCORE_ROW + PAD, :] = score


def add_kernel(kept_ref, got_ref, *outs):
    row = lax.broadcasted_iota(jnp.int32, (PAD, GROUP_WIDTH), 0)
    for j, out in zip(range(1, SLOTS), outs):
        base = j * (SCORE_ROW + PAD)
        total = kept_ref[base : base + SCORE_ROW + PAD, :] + got_ref[base : base + SCORE_ROW + PAD, :]
        out[0:SCORE_ROW, :] = total[0:SCORE_ROW].astype(BF)
        a, b = (jnp.broadcast_to(v.astype(F32)[0:1], row.shape) for v in two_terms(total[SCORE_ROW:]))
        if out.shape[0] > HALO_ROW:
            out[HALO_ROW:, :] = jnp.zeros((out.shape[0] - HALO_ROW, GROUP_WIDTH), BF)
        out[SCORE_ROW:HALO_ROW, :] = jnp.where(row == 0, a, jnp.where(row == 1, b, 0.0)).astype(BF)


def input_half(files, stream, hg_ref, hx_ref, message, w_refs, out):
    rows = hg_ref.shape[1]
    since, _ = row_info(message, files, 0, rows + PAD)
    for j in range(SLOTS):
        halves = kernel_halves(w_refs, j)
        ahead = hx_ref[stream, :, lanes(j)].astype(F32)[PAD:]
        grad = jnp.concatenate([hg_ref[stream, :, lanes(j)].astype(F32), ahead], axis=0)
        total = jnp.zeros((rows + PAD, GROUP_WIDTH), F32)
        for lag in range(KERNEL):
            window = grad if lag == 0 else jnp.where(since >= lag, grad, 0.0)
            if lag > 0:
                window = pltpu.roll(window, rows + PAD - lag, 0)
            part = halves[lag // 2][GROUP_WIDTH * (lag % 2) : GROUP_WIDTH * (lag % 2 + 1)]
            total = total + nt(window.astype(BF), part)
        out[:, lanes(j)] = total[:rows].astype(BF)


def send_kernel(files, hg_ref, hx_ref, other_ref, wm_ref, wt_ref, out):
    input_half(files, 1, hg_ref, hx_ref, other_ref, (wm_ref, wt_ref), out)


def own_kernel(files, hg_ref, hx_ref, mine_ref, wm_ref, wt_ref, x_out, value_ref, sems):
    input_half(files, 0, hg_ref, hx_ref, mine_ref, (wm_ref, wt_ref), value_ref)
    for copy in half_copies(value_ref, x_out, lax.axis_index("dp"), sems):
        copy.wait()


def half_copies(value_ref, x_out, parity, sems):
    s = lax.axis_index("seq")
    copies = [
        pltpu.make_async_copy(
            value_ref.at[:, lanes(j)],
            x_out.at[0, :, group_lanes(slot_group(s, j, parity))],
            sems.at[j],
        )
        for j in range(SLOTS)
    ]
    for copy in copies:
        copy.start()
    return copies


def finish_kernel(kept_ref, got_ref, z1, z2, z3, x_got_ref, x_hbm,
                  x_out, grad_out, score_out, grad_ref, score_ref, sems):
    del x_hbm
    f = lax.axis_index("fsdp")
    copies = half_copies(x_got_ref, x_out, 1 - lax.axis_index("dp"), sems)
    total = kept_ref[0 : SCORE_ROW + PAD, :] + got_ref[0 : SCORE_ROW + PAD, :]
    grad, score = total[0:SCORE_ROW], total[SCORE_ROW:]
    for ref in (z1, z2, z3):
        grad = grad + ref[0:SCORE_ROW, :].astype(F32)
        pair = ref[SCORE_ROW:HALO_ROW, :].astype(F32)
        score = score + jnp.sum(pair, axis=0, keepdims=True)
    grad_ref[...] = grad
    copy_grad = pltpu.make_async_copy(grad_ref, grad_out, sems.at[SLOTS])
    copy_grad.start()
    half = GROUP_WIDTH // 2
    score_ref[...] = jnp.where(
        jnp.full((1, half), f, jnp.int32) == 0, score[0:1, :half], score[0:1, half:]
    )
    copy_score = pltpu.make_async_copy(score_ref, score_out, sems.at[SLOTS + 1])
    copy_score.start()
    for copy in copies + [copy_grad, copy_score]:
        copy.wait()


def per_device_paired(inputs, conv_weight, score_weight, lengths, offsets, cotangent):
    rows, pairs, files = inputs.shape[1], cotangent.shape[1], offsets.shape[1]
    shape = jax.ShapeDtypeStruct

    def flip(value, axis):
        return lax.ppermute(value, axis, [(0, 1), (1, 0)])

    def cycle(value, by):
        return lax.ppermute(value, "seq", [(i, (i + by) % SLOTS) for i in range(SLOTS)])

    message = shape((rows + pairs + PAD, HALF), BF)
    mine, other, mw1, mw2, mw3 = call(
        pack_kernel,
        (
            message,
            message,
            shape((HALO_ROW + 2 * PAD * SLOTS + SPARE, GROUP_WIDTH), BF),
            shape((HALO_ROW, GROUP_WIDTH), BF),
            shape((HALO_ROW + 2 * PAD * SLOTS, GROUP_WIDTH), BF),
        ),
        scratch=(
            pltpu.SMEM(offsets.shape, jnp.int32),
            pltpu.VMEM(inputs.shape, BF),
            pltpu.VMEM(cotangent.shape, BF),
            pltpu.VMEM((1, score_weight.shape[0]), BF),
            pltpu.SemaphoreType.DMA((7,)),
        ),
        hbm=5,
    )(*(pltpu.with_memory_space_constraint(v, pltpu.HBM) for v in (offsets, inputs, cotangent, conv_weight, score_weight.reshape(1, -1))), lengths.reshape(1, 1))
    other = flip(other, "dp")
    halo = shape((2 * PAD, HALF), BF)
    kernel_mine, halo_own, halo_other = call(
        join_kernel, (shape((SLOTS * SHARD + JOINED_SPARE, GROUP_WIDTH), BF), halo, halo)
    )(mw2, cycle(mw1, 1), cycle(mw2, 2), cycle(mw3, 3))
    halo_other = flip(halo_other, "dp")
    shards = (kernel_mine, flip(kernel_mine, "fsdp"))
    left = shape((2, pairs + PAD, HALF), BF)
    sums = shape((2, 16, GROUP_WIDTH), F32)
    hidden, left_main, partial = call(
        functools.partial(hidden_kernel, files), (shape((2, rows, HALF), F32), left, sums)
    )(mine, other, *shards)
    edge_hidden, left, partial = call(
        functools.partial(edge_hidden_kernel, files),
        (shape((2, 2 * PAD, HALF), F32), left, sums),
    )(mine, other, halo_own, halo_other, *shards, left_main, partial)
    partial_r = flip(partial, "dp")
    windows = call(
        functools.partial(window_kernel, files),
        shape((SLOTS, KERNEL * GROUP_WIDTH, 2 * (rows + 2 * PAD)), BF),
        cost=pl.CostEstimate(flops=0, transcendentals=0, bytes_accessed=2 * 1024 * 1024),
    )(mine, other, halo_own, halo_other, partial)
    grad_rows = SLOTS * (SCORE_ROW + PAD)
    hg, hg_ahead, kept, send = call(
        functools.partial(mix_kernel, files),
        (
            shape((2, rows, HALF), BF),
            shape((2, 2 * PAD, HALF), BF),
            shape((grad_rows, GROUP_WIDTH), F32),
            shape((grad_rows, GROUP_WIDTH), F32),
        ),
    )(mine, other, windows, hidden, edge_hidden, left, partial, partial_r)
    got = flip(send, "fsdp")
    x_send = call(functools.partial(send_kernel, files), shape((rows, HALF), BF))(
        hg, hg_ahead, other, *shards
    )
    x_got = flip(x_send, "dp")
    summed = shape((HALO_ROW, GROUP_WIDTH), BF)
    first = shape((HALO_ROW + PAD, GROUP_WIDTH), BF)
    sums = call(add_kernel, tuple(first if j == 2 else summed for j in range(1, SLOTS)))(kept, got)
    final = [cycle(value, -j) for j, value in zip(range(1, SLOTS), sums)]
    vmem, hbm = pl.BlockSpec(memory_space=pltpu.VMEM), pl.BlockSpec(memory_space=pltpu.HBM)
    params = pltpu.CompilerParams(vmem_limit_bytes=48 * 1024 * 1024)
    input_grad = pl.pallas_call(
        functools.partial(own_kernel, files),
        out_shape=shape(inputs.shape, BF),
        in_specs=[vmem] * 5,
        out_specs=hbm,
        scratch_shapes=[pltpu.VMEM((rows, HALF), BF), pltpu.SemaphoreType.DMA((SLOTS,))],
        compiler_params=params,
        cost_estimate=pl.CostEstimate(flops=0, transcendentals=0, bytes_accessed=4 * 1024 * 1024),
    )(hg, hg_ahead, mine, *shards)
    input_grad, kernel_grad, score_grad = pl.pallas_call(
        finish_kernel,
        out_shape=(
            shape(inputs.shape, BF),
            shape((SCORE_ROW, GROUP_WIDTH), F32),
            shape((1, GROUP_WIDTH // 2), F32),
        ),
        in_specs=[vmem] * 6 + [hbm],
        out_specs=(hbm, hbm, hbm),
        scratch_shapes=[
            pltpu.VMEM((SCORE_ROW, GROUP_WIDTH), F32),
            pltpu.VMEM((1, GROUP_WIDTH // 2), F32),
            pltpu.SemaphoreType.DMA((SLOTS + 2,)),
        ],
        input_output_aliases={6: 0},
        compiler_params=params,
    )(kept, got, *final, x_got, input_grad)
    return (input_grad, kernel_grad, score_grad.reshape(-1))


def solution(mesh):
    placed = (
        P(("parts", "dp", "fsdp"), "seq", None),
        P(("seq", "dp", "fsdp"), None),
        P(("seq", "dp", "fsdp")),
        P(("parts", "dp", "fsdp")),
        P(("parts", "dp", "fsdp"), None),
        P(("parts", "dp", "fsdp"), "seq", None),
    )
    paired = mesh.shape["seq"] == SLOTS and mesh.shape["dp"] == 2 and mesh.shape["fsdp"] == 2
    return jax.shard_map(
        per_device_paired if paired else per_device_general,
        mesh=mesh,
        in_specs=placed,
        out_specs=(
            P(("parts", "dp", "fsdp"), "seq", None),
            P(("parts", "seq", "dp", "fsdp"), None),
            P(("parts", "seq", "dp", "fsdp")),
        ),
        check_vma=False,
    )
```

```python
import functools

import jax
import jax.numpy as jnp
from jax import lax
from jax.experimental import pallas as pl
from jax.experimental.pallas import tpu as pltpu
from jax.sharding import PartitionSpec as P

GROUPS = 8
KERNEL = 4
GROUP_WIDTH = 128


precise_mode = lax.Precision.HIGHEST


def shifted(value, axis, by):
    devices = lax.axis_size(axis)
    pairs = [(i, i + by) for i in range(devices) if 0 <= i + by < devices]
    return lax.ppermute(value, axis, pairs)


def segment_of(positions, offsets):
    return jnp.sum((offsets[None, :] <= positions[:, None]).astype(jnp.int32), axis=1)


def tap_valid(positions, offsets, lag_steps):
    earlier = positions - lag_steps
    same_file = segment_of(positions, offsets) == segment_of(earlier, offsets)
    return jnp.logical_and(earlier >= 0, same_file)


def mix_backward(hidden, upstream, score_vec):
    row_count = hidden.shape[0]
    width_all = hidden.shape[1]
    pooled_list = []
    logit_list = []
    for block_size in range(1, 5):
        pooled = hidden.reshape(row_count // block_size, block_size, width_all).sum(axis=1) * (
            1.0 / block_size
        )
        pooled_list.append(pooled)
        logit_list.append(
            jnp.repeat(jnp.dot(pooled, score_vec, precision=precise_mode), block_size)
        )
    logits = jnp.stack(logit_list)
    exp_logits = jnp.exp(logits)
    choose_prob = exp_logits / jnp.sum(exp_logits, axis=0)
    mix_grad = jnp.repeat(upstream.astype(jnp.float32) * 0.5, 2, axis=0)
    inner_list = []
    for block_size in range(1, 5):
        pooled = pooled_list[block_size - 1]
        inner = jnp.sum(
            mix_grad.reshape(row_count // block_size, block_size, width_all) * pooled[:, None, :],
            axis=2,
        )
        inner_list.append(inner.reshape(row_count))
    inner_all = jnp.stack(inner_list)
    dlogit = choose_prob * (inner_all - jnp.sum(choose_prob * inner_all, axis=0))
    hidden_grad = jnp.zeros((row_count, width_all), jnp.float32)
    weight_grad = jnp.zeros((width_all,), jnp.float32)
    for block_size in range(1, 5):
        block_logit = (
            dlogit[block_size - 1].reshape(row_count // block_size, block_size).sum(axis=1)
        )
        block_mix = (
            (choose_prob[block_size - 1][:, None] * mix_grad)
            .reshape(row_count // block_size, block_size, width_all)
            .sum(axis=1)
        )
        block_term = (block_mix + block_logit[:, None] * score_vec[None, :]) * (1.0 / block_size)
        hidden_grad = hidden_grad + jnp.repeat(block_term, block_size, axis=0)
        weight_grad = weight_grad + jnp.dot(
            block_logit, pooled_list[block_size - 1], precision=precise_mode
        )
    return (hidden_grad, weight_grad)


def per_device_general(inputs, conv_weight, score_weight, lengths, offsets, cotangent):
    local_rows = inputs.shape[1]
    width_all = inputs.shape[2]
    kernel_flat, score_full = (
        lax.all_gather(conv_weight, ("seq", "dp", "fsdp"), axis=0, tiled=True),
        lax.all_gather(score_weight, ("seq", "dp", "fsdp"), axis=0, tiled=True),
    )
    kernel_full = kernel_flat.reshape(GROUPS, KERNEL, GROUP_WIDTH, GROUP_WIDTH)
    score_vec = score_full.astype(jnp.float32)
    start_row = lax.axis_index("seq") * local_rows
    positions = start_row + jnp.arange(local_rows, dtype=jnp.int32)
    own_rows = inputs[0]
    file_starts = offsets[0]
    valid = (positions < lengths[0]).astype(jnp.float32)
    left_rows = shifted(own_rows[local_rows - (KERNEL - 1) :], "seq", 1)
    padded = jnp.concatenate([left_rows, own_rows], axis=0)
    windows = []
    hidden = jnp.zeros((local_rows, GROUPS, GROUP_WIDTH), jnp.float32)
    for tap_index in range(KERNEL):
        window = padded[KERNEL - 1 - tap_index : KERNEL - 1 - tap_index + local_rows]
        keep = tap_valid(positions, file_starts, tap_index)
        window = jnp.where(keep[:, None], window, jnp.zeros_like(window)).reshape(
            local_rows, GROUPS, GROUP_WIDTH
        )
        windows.append(window)
        hidden = hidden + jnp.einsum(
            "ngc,gco->ngo", window, kernel_full[:, tap_index], preferred_element_type=jnp.float32
        )
    hidden = hidden.reshape(local_rows, width_all) * valid[:, None]
    hidden_grad, weight_grad = mix_backward(hidden, cotangent[0], score_vec)
    hidden_low = (hidden_grad * valid[:, None]).astype(jnp.bfloat16)
    right_rows = shifted(hidden_low[: KERNEL - 1], "seq", -1)
    grad_padded = jnp.concatenate([hidden_low, right_rows], axis=0)
    hidden_groups = hidden_low.reshape(local_rows, GROUPS, GROUP_WIDTH)
    input_grad = jnp.zeros((local_rows, GROUPS, GROUP_WIDTH), jnp.float32)
    kernel_terms = []
    for tap_index in range(KERNEL):
        window = grad_padded[tap_index : tap_index + local_rows]
        keep = tap_valid(positions + tap_index, file_starts, tap_index)
        window = jnp.where(keep[:, None], window, jnp.zeros_like(window)).reshape(
            local_rows, GROUPS, GROUP_WIDTH
        )
        input_grad = input_grad + jnp.einsum(
            "ngo,gco->ngc", window, kernel_full[:, tap_index], preferred_element_type=jnp.float32
        )
        kernel_terms.append(
            jnp.einsum(
                "ngc,ngo->gco",
                windows[tap_index],
                hidden_groups,
                preferred_element_type=jnp.float32,
            )
        )
    input_grad = input_grad.reshape(local_rows, width_all).astype(jnp.bfloat16)[None]
    kernel_part = jnp.stack(kernel_terms, axis=1).reshape(
        GROUPS * KERNEL * GROUP_WIDTH, GROUP_WIDTH
    )
    kernel_grad, score_grad = (
        lax.psum_scatter(kernel_part, ("seq", "dp", "fsdp"), scatter_dimension=0, tiled=True),
        lax.psum_scatter(weight_grad, ("seq", "dp", "fsdp"), scatter_dimension=0, tiled=True),
    )
    return (input_grad, kernel_grad, score_grad)


SLOTS = 4
HALF = SLOTS * GROUP_WIDTH
PAD = 8
SCORE_ROW = 2 * GROUP_WIDTH
HALO_ROW = SCORE_ROW + PAD
SHARD = SCORE_ROW + 2 * PAD
AHEAD = 4
HEAD = 6
SPARE = 0
JOINED_SPARE = 64
BF = jnp.bfloat16
F32 = jnp.float32


def lanes(slot):
    return slice(slot * GROUP_WIDTH, (slot + 1) * GROUP_WIDTH)


def group_lanes(group):
    return pl.ds(pl.multiple_of(group * GROUP_WIDTH, GROUP_WIDTH), GROUP_WIDTH)


def slot_group(seq, slot, parity):
    return 2 * lax.rem(seq - slot + 2 * SLOTS, SLOTS) + parity


def call(body, out_shape, scratch=(), hbm=0, cost=None):
    def run(*args):
        specs = [pl.BlockSpec(memory_space=pltpu.HBM)] * hbm
        specs += [pl.BlockSpec(memory_space=pltpu.VMEM)] * (len(args) - hbm)
        return pl.pallas_call(
            body,
            out_shape=out_shape,
            in_specs=specs,
            out_specs=jax.tree.map(lambda _: pl.BlockSpec(memory_space=pltpu.VMEM), out_shape),
            scratch_shapes=list(scratch),
            cost_estimate=cost,
            compiler_params=pltpu.CompilerParams(vmem_limit_bytes=48 * 1024 * 1024),
        )(*args)

    return run


def appended(half, slot):
    first = HALO_ROW + PAD * (SLOTS * half + slot)
    return slice(first, first + PAD)


def pack_kernel(off_hbm, x_hbm, c_hbm, w_hbm, score_hbm, len_ref, mine, other, mw1, mw2, mw3,
                off_ref, x_ref, c_ref, score_ref, sems):
    rows, pairs, files = x_ref.shape[1], c_ref.shape[1], off_ref.shape[1]
    s, d, f = (lax.axis_index(name) for name in ("seq", "dp", "fsdp"))
    copies = [
        pltpu.make_async_copy(source, target, sems.at[i])
        for i, (source, target) in enumerate(
            (
                (x_hbm, x_ref),
                (c_hbm, c_ref),
                (off_hbm, off_ref),
                (score_hbm, score_ref),
                (w_hbm, mw2.at[0:SCORE_ROW]),
            )
        )
    ]
    for copy in copies:
        copy.start()
    for copy in copies[2:4]:
        copy.wait()
    lane = lax.broadcasted_iota(jnp.int32, (PAD, GROUP_WIDTH), 1)
    tile_row = lax.broadcasted_iota(jnp.int32, (PAD, GROUP_WIDTH), 0)
    start = s * rows
    info = jnp.zeros((PAD, GROUP_WIDTH), jnp.int32)
    for i in range(files):
        info = jnp.where(lane == i, jnp.clip(off_ref[0, i] - start, -4, rows + PAD), info)
    info = jnp.where(lane == files, jnp.clip(len_ref[0:1, 0:1] - start, 0, rows + PAD), info)
    info = (info.astype(F32) * 0.25).astype(BF)
    value = score_ref[...].astype(F32)
    both = jnp.concatenate([value, value], axis=1)
    keep = (lane // (GROUP_WIDTH // 2) == f) & (tile_row == 0)
    block = jnp.where(keep, jnp.broadcast_to(both, (PAD, GROUP_WIDTH)), 0.0)
    for ref in (mw1, mw2, mw3):
        ref[SCORE_ROW:HALO_ROW, :] = block.astype(BF)
    if SPARE:
        mw1[HALO_ROW + 2 * PAD * SLOTS :, :] = jnp.zeros((SPARE, GROUP_WIDTH), BF)
    copies[0].wait()
    for ref, parity in ((other, 1 - d), (mine, d)):
        for j in range(SLOTS):
            ref[0:rows, lanes(j)] = x_ref[0, :, group_lanes(slot_group(s, j, parity))]
    for half, parity in ((0, d), (1, 1 - d)):
        for j in range(SLOTS):
            after = group_lanes(slot_group(s + 1, j, parity))
            mw1[appended(half, j), :] = x_ref[0, rows - PAD :, after]
    copies[1].wait()
    for ref, parity in ((other, 1 - d), (mine, d)):
        for j in range(SLOTS):
            col = group_lanes(slot_group(s, j, parity))
            ref[rows : rows + pairs, lanes(j)] = c_ref[0, :, col]
        ref[rows + pairs :, :] = jnp.zeros((PAD, HALF), BF)
        ref[rows + pairs :, lanes(0)] = info
    for half, parity in ((0, d), (1, 1 - d)):
        for j in range(SLOTS):
            before = group_lanes(slot_group(s - 1, j, parity))
            moved = pltpu.roll(c_ref[0, 0:PAD, before].astype(F32), HEAD, 0)
            head = jnp.where(tile_row < HEAD, x_ref[0, 0:PAD, before].astype(F32), moved)
            mw3[appended(half, j), :] = head.astype(BF)
    copies[4].wait()
    for ref in (mw1, mw3):
        ref[0:SCORE_ROW, :] = mw2[0:SCORE_ROW, :]


def join_kernel(w0, w1, w2, w3, joined, halo_own, halo_flip):
    if JOINED_SPARE:
        joined[SLOTS * SHARD :, :] = jnp.zeros((JOINED_SPARE, GROUP_WIDTH), BF)
    none = jnp.zeros((SHARD - HALO_ROW, GROUP_WIDTH), F32)
    for j, ref in enumerate((w0, w1, w2, w3)):
        joined[SHARD * j : SHARD * j + SCORE_ROW, :] = ref[0:SCORE_ROW, :]
        score = jnp.concatenate([ref[SCORE_ROW:HALO_ROW, :].astype(F32), none], axis=0)
        joined[SHARD * j + SCORE_ROW : SHARD * (j + 1), :] = score.astype(BF)
    for half, out in enumerate((halo_own, halo_flip)):
        for j in range(SLOTS):
            out[0:PAD, lanes(j)] = w1[appended(half, j), :]
            out[PAD:, lanes(j)] = w3[appended(half, j), :]


def row_info(message, files, first, count):
    info = message[message.shape[0] - PAD :, lanes(0)].astype(F32)[0:1] * 4.0
    lane = lax.broadcasted_iota(jnp.int32, (1, GROUP_WIDTH), 1)
    length = jnp.sum(jnp.where(lane == files, info, 0.0), axis=1, keepdims=True)
    pos = lax.broadcasted_iota(jnp.int32, (count, GROUP_WIDTH), 0).astype(F32) + first
    starts = jnp.where((lane < files) & (info <= pos), info, -4096.0)
    since = pos - jnp.max(starts, axis=1, keepdims=True)
    return since, (pos < length).astype(F32)


def block_weights(count, ahead=0, start=0):
    q = lax.broadcasted_iota(jnp.int32, (count, GROUP_WIDTH), 0)
    r = lax.broadcasted_iota(jnp.int32, (count, GROUP_WIDTH), 1)
    if ahead:
        q = jnp.where(q < start, q, q + (ahead - start))

    def over(value, size):
        if size == 1:
            return value
        if size == 3:
            return lax.shift_right_logical(value * 21846, 16)
        return lax.shift_right_logical(value, size // 2)

    return [
        [
            jnp.where(over(q, size) == over(2 * r + odd, size), 1.0 / size, 0.0).astype(F32)
            for size in range(1, 5)
        ]
        for odd in range(2)
    ]


def message_rows(message):
    return (message.shape[0] - PAD) // 3 * 2


def windows_of(message, tail, j, since):
    value = message[0 : message_rows(message), lanes(j)]
    padded = jnp.concatenate([tail.astype(F32), value.astype(F32)], axis=0)
    out = [value]
    for lag in range(1, KERNEL):
        moved = pltpu.roll(padded, lag, 0)[PAD:]
        out.append(jnp.where(since >= lag, moved, 0.0).astype(BF))
    return out


def edge_windows_of(message, halo_ref, j, since):
    rows = message_rows(message)
    none = jnp.zeros((PAD, GROUP_WIDTH), F32)
    halo = halo_ref[:, lanes(j)].astype(F32)
    last = message[rows - 2 * PAD : rows, lanes(j)].astype(F32)[PAD:]
    before = jnp.concatenate([halo[:PAD], none], axis=0)
    after = jnp.concatenate([last, halo[PAD:]], axis=0)
    out = []
    for lag in range(KERNEL):
        shift = [pltpu.roll(v, lag, 0)[PAD:] if lag else v[PAD:] for v in (before, after)]
        moved = jnp.concatenate(shift, axis=0)
        out.append(jnp.where(since >= lag, moved, 0.0).astype(BF))
    return out


def kernel_rows(w_refs, j):
    return jnp.concatenate(kernel_halves(w_refs, j), axis=0)


def kernel_halves(w_refs, j):
    f = lax.axis_index("fsdp")
    mine, theirs = (ref[SHARD * j : SHARD * j + SCORE_ROW, :] for ref in w_refs)
    first = jnp.full((SCORE_ROW, GROUP_WIDTH), f, jnp.int32) == 0
    return jnp.where(first, mine, theirs), jnp.where(first, theirs, mine)


def nt(a, b):
    return lax.dot_general(a, b, (((1,), (1,)), ((), ())), preferred_element_type=F32)


def two_terms(value):
    high = value.astype(BF)
    return high, (value - high.astype(F32)).astype(BF)


def gram_of(hidden, left):
    a, b = two_terms(hidden)
    return nt(a, left) + nt(b, left)


def block_sums(weights, gram, column):
    inner = [
        jnp.sum(weights[odd][b] * gram, axis=0, keepdims=True) * 0.5
        for odd in range(2)
        for b in range(4)
    ]
    logit = [
        jnp.sum(weights[odd][b] * column, axis=0, keepdims=True)
        for odd in range(2)
        for b in range(4)
    ]
    return jnp.concatenate(inner + logit, axis=0)


def own_window_kernel(files, message, out_ref):
    since, _ = row_info(message, files, 0, message_rows(message))
    none = jnp.zeros((PAD, GROUP_WIDTH), F32)
    for j in range(SLOTS):
        out_ref[j] = jnp.concatenate(windows_of(message, none, j, since), axis=1)


def hidden_kernel(files, own_win, mine_ref, other_ref, wm_ref, wt_ref, h_out, l_out, r_out):
    messages = (mine_ref, other_ref)
    rows = h_out.shape[1]
    pairs = rows // 2
    infos = [row_info(ref, files, 0, rows) for ref in messages]
    row = lax.broadcasted_iota(jnp.int32, (PAD, GROUP_WIDTH), 0)
    none = jnp.zeros((PAD, GROUP_WIDTH), F32)
    for j in range(SLOTS):
        kernel = kernel_rows((wm_ref, wt_ref), j)
        score_rows = slice(SHARD * j + SCORE_ROW, SHARD * (j + 1))
        score = wm_ref[score_rows, :].astype(F32) + wt_ref[score_rows, :].astype(F32)
        score = jnp.where(row == AHEAD, jnp.broadcast_to(score[0:1], row.shape), 0.0)
        for stream in range(2):
            since, valid = infos[stream]
            if stream == 0:
                win = own_win[j]
            else:
                win = jnp.concatenate(windows_of(messages[stream], none, j, since), axis=1)
            hidden = jnp.dot(win, kernel, preferred_element_type=F32)
            h_out[stream, :, lanes(j)] = hidden * valid
            cot = messages[stream][rows : rows + pairs, lanes(j)]
            left = jnp.concatenate([cot.astype(F32), score], axis=0).astype(BF)
            l_out[stream, :, lanes(j)] = left
    weights = block_weights(rows)
    scored = pairs + AHEAD
    for stream in range(2):
        gram = gram_of(h_out[stream], l_out[stream])
        r_out[stream] = block_sums(weights, gram, gram[:, scored : scored + 1])


def edge_info(message, files):
    rows = message_rows(message)
    first, ahead = row_info(message, files, 0, PAD), row_info(message, files, rows, PAD)
    return [jnp.concatenate(pair, axis=0) for pair in zip(first, ahead)]


def edge_hidden_kernel(files, mine_ref, other_ref, own_halo, other_halo, wm_ref, wt_ref, l_ref,
                       r_ref, h_out, l_out, r_out):
    messages, halos = (mine_ref, other_ref), (own_halo, other_halo)
    rows = message_rows(mine_ref)
    kept = rows // 2 - PAD
    infos = [edge_info(ref, files) for ref in messages]
    row = lax.broadcasted_iota(jnp.int32, (2 * PAD, GROUP_WIDTH), 0)
    for stream in range(2):
        l_out[stream, 0:kept, :] = l_ref[stream, 0:kept, :]
    for j in range(SLOTS):
        kernel = kernel_rows((wm_ref, wt_ref), j)
        wins = [
            jnp.concatenate(edge_windows_of(messages[i], halos[i], j, infos[i][0]), axis=1)
            for i in range(2)
        ]
        hidden = jnp.dot(jnp.concatenate(wins, axis=0), kernel, preferred_element_type=F32)
        for stream in range(2):
            block = hidden[2 * PAD * stream : 2 * PAD * (stream + 1)]
            h_out[stream, :, lanes(j)] = block * infos[stream][1]
            head = halos[stream][:, lanes(j)].astype(F32)
            head = pltpu.roll(head, 2 * PAD - HEAD, 0)
            old = l_ref[stream, kept:, lanes(j)].astype(F32)
            take = (row >= PAD) & (row < PAD + 2)
            l_out[stream, kept:, lanes(j)] = jnp.where(take, head, old).astype(BF)
    weights = block_weights(2 * PAD, rows, PAD)
    scored = rows // 2 + AHEAD
    for stream in range(2):
        gram = gram_of(h_out[stream], l_out[stream])
        column = gram[:, scored : scored + 1]
        r_out[stream] = r_ref[stream] + block_sums(weights, gram, column)


def window_kernel(files, mine_ref, other_ref, own_halo, other_halo, after_ref, out_ref):
    del after_ref
    for stream, (message, halo) in enumerate(((mine_ref, own_halo), (other_ref, other_halo))):
        since, _ = row_info(message, files, 0, message_rows(message))
        for j in range(SLOTS):
            win = windows_of(message, halo[0:PAD, lanes(j)], j, since)
            for lag in range(KERNEL):
                value = jnp.concatenate([win[lag], jnp.zeros((2 * PAD, GROUP_WIDTH), BF)], axis=0)
                span = value.shape[0]
                out_ref[j, lanes(lag), span * stream : span * (stream + 1)] = value.T


def mixing(weights, total, count):
    spread = jnp.zeros((count, GROUP_WIDTH), F32)
    carry = jnp.zeros((count, GROUP_WIDTH), F32)
    for odd in range(2):
        for b in range(4):
            choose, change = total[odd][b]
            spread = spread + weights[odd][b] * choose
            carry = carry + weights[odd][b] * change
    return spread, jnp.sum(carry, axis=1, keepdims=True)


def mix_kernel(files, mine_ref, other_ref, win_ref, h_ref, he_ref, l_ref, r_ref, rr_ref,
               hg_out, hx_out, mine_out, send_out):
    messages = (mine_ref, other_ref)
    rows = h_ref.shape[1]
    scored = rows // 2 + AHEAD
    f = lax.axis_index("fsdp")
    weights = block_weights(rows)
    edge_weights = block_weights(2 * PAD, rows, PAD)
    columns = []
    for stream in range(2):
        summed = r_ref[stream] + rr_ref[1 - stream]
        total = []
        for odd in range(2):
            inner = [summed[4 * odd + b : 4 * odd + b + 1] for b in range(4)]
            logit = [summed[8 + 4 * odd + b : 8 + 4 * odd + b + 1] for b in range(4)]
            top = jnp.maximum(jnp.maximum(logit[0], logit[1]), jnp.maximum(logit[2], logit[3]))
            powers = [jnp.exp(v - top) for v in logit]
            scale = 1.0 / (powers[0] + powers[1] + powers[2] + powers[3])
            choose = [v * scale for v in powers]
            mean = sum(c * m for c, m in zip(choose, inner))
            total.append([(c * 0.5, c * (m - mean)) for c, m in zip(choose, inner)])
        parts = (
            (weights, rows, row_info(messages[stream], files, 0, rows)[1]),
            (edge_weights, 2 * PAD, edge_info(messages[stream], files)[1]),
        )
        terms = []
        for part_weights, count, valid in parts:
            spread, e = mixing(part_weights, total, count)
            lane = lax.broadcasted_iota(jnp.int32, (count, GROUP_WIDTH), 1)
            terms.append(two_terms(jnp.where(lane == scored, e, spread) * valid))
            if count == rows:
                columns.append(e)
        left = l_ref[stream]
        grad = jnp.dot(
            jnp.concatenate([jnp.concatenate(pair, axis=1) for pair in terms], axis=0),
            jnp.concatenate([left, left], axis=0),
            preferred_element_type=F32,
        ).astype(BF)
        hg_out[stream] = grad[:rows]
        hx_out[stream] = grad[rows:]
    first = jnp.full((SCORE_ROW, GROUP_WIDTH), f, jnp.int32) == 0
    row = lax.broadcasted_iota(jnp.int32, (PAD, GROUP_WIDTH), 0)
    for j in range(SLOTS):
        none = jnp.zeros((2 * PAD, GROUP_WIDTH), BF)
        grads = [v for i in range(2) for v in (hg_out[i, :, lanes(j)], none)]
        both = jnp.dot(
            win_ref[j], jnp.concatenate(grads, axis=0), preferred_element_type=F32
        )
        low, high = both[:SCORE_ROW], both[SCORE_ROW:]
        score = jnp.zeros((1, GROUP_WIDTH), F32)
        for stream in range(2):
            value = columns[stream] * h_ref[stream, :, lanes(j)]
            edge = columns[stream][0:PAD] * he_ref[stream, 0:PAD, lanes(j)]
            score = score + jnp.sum(value, axis=0, keepdims=True)
            score = score + jnp.sum(edge, axis=0, keepdims=True)
        base = j * (SCORE_ROW + PAD)
        score = jnp.where(row == 0, jnp.broadcast_to(score, row.shape), 0.0)
        mine_out[base : base + SCORE_ROW, :] = jnp.where(first, low, high)
        send_out[base : base + SCORE_ROW, :] = jnp.where(first, high, low)
        mine_out[base + SCORE_ROW : base + SCORE_ROW + PAD, :] = score
        send_out[base + SCORE_ROW : base + SCORE_ROW + PAD, :] = score


def add_kernel(kept_ref, got_ref, *outs):
    row = lax.broadcasted_iota(jnp.int32, (PAD, GROUP_WIDTH), 0)
    for j, out in zip(range(1, SLOTS), outs):
        base = j * (SCORE_ROW + PAD)
        total = kept_ref[base : base + SCORE_ROW + PAD, :] + got_ref[base : base + SCORE_ROW + PAD, :]
        out[0:SCORE_ROW, :] = total[0:SCORE_ROW].astype(BF)
        a, b = (jnp.broadcast_to(v.astype(F32)[0:1], row.shape) for v in two_terms(total[SCORE_ROW:]))
        if out.shape[0] > HALO_ROW:
            out[HALO_ROW:, :] = jnp.zeros((out.shape[0] - HALO_ROW, GROUP_WIDTH), BF)
        out[SCORE_ROW:HALO_ROW, :] = jnp.where(row == 0, a, jnp.where(row == 1, b, 0.0)).astype(BF)


def input_half(files, stream, hg_ref, hx_ref, message, w_refs, out):
    rows = hg_ref.shape[1]
    since, _ = row_info(message, files, 0, rows + PAD)
    for j in range(SLOTS):
        halves = kernel_halves(w_refs, j)
        ahead = hx_ref[stream, :, lanes(j)].astype(F32)[PAD:]
        grad = jnp.concatenate([hg_ref[stream, :, lanes(j)].astype(F32), ahead], axis=0)
        total = jnp.zeros((rows + PAD, GROUP_WIDTH), F32)
        for lag in range(KERNEL):
            window = grad if lag == 0 else jnp.where(since >= lag, grad, 0.0)
            if lag > 0:
                window = pltpu.roll(window, rows + PAD - lag, 0)
            part = halves[lag // 2][GROUP_WIDTH * (lag % 2) : GROUP_WIDTH * (lag % 2 + 1)]
            total = total + nt(window.astype(BF), part)
        out[:, lanes(j)] = total[:rows].astype(BF)


def send_kernel(files, hg_ref, hx_ref, other_ref, wm_ref, wt_ref, out):
    input_half(files, 1, hg_ref, hx_ref, other_ref, (wm_ref, wt_ref), out)


def own_kernel(files, hg_ref, hx_ref, mine_ref, wm_ref, wt_ref, x_out, value_ref, sems):
    input_half(files, 0, hg_ref, hx_ref, mine_ref, (wm_ref, wt_ref), value_ref)
    for copy in half_copies(value_ref, x_out, lax.axis_index("dp"), sems):
        copy.wait()


def half_copies(value_ref, x_out, parity, sems):
    s = lax.axis_index("seq")
    copies = [
        pltpu.make_async_copy(
            value_ref.at[:, lanes(j)],
            x_out.at[0, :, group_lanes(slot_group(s, j, parity))],
            sems.at[j],
        )
        for j in range(SLOTS)
    ]
    for copy in copies:
        copy.start()
    return copies


def place_kernel(x_got_ref, x_hbm, x_out, sems):
    del x_hbm
    for copy in half_copies(x_got_ref, x_out, 1 - lax.axis_index("dp"), sems):
        copy.wait()


def finish_kernel(kept_ref, got_ref, z1, z2, z3, grad_out, score_out, grad_ref, score_ref, sems):
    f = lax.axis_index("fsdp")
    total = kept_ref[0 : SCORE_ROW + PAD, :] + got_ref[0 : SCORE_ROW + PAD, :]
    grad, score = total[0:SCORE_ROW], total[SCORE_ROW:]
    for ref in (z1, z2, z3):
        grad = grad + ref[0:SCORE_ROW, :].astype(F32)
        pair = ref[SCORE_ROW:HALO_ROW, :].astype(F32)
        score = score + jnp.sum(pair, axis=0, keepdims=True)
    grad_ref[...] = grad
    copy_grad = pltpu.make_async_copy(grad_ref, grad_out, sems.at[0])
    copy_grad.start()
    half = GROUP_WIDTH // 2
    score_ref[...] = jnp.where(
        jnp.full((1, half), f, jnp.int32) == 0, score[0:1, :half], score[0:1, half:]
    )
    copy_score = pltpu.make_async_copy(score_ref, score_out, sems.at[1])
    copy_score.start()
    for copy in (copy_grad, copy_score):
        copy.wait()


def per_device_paired(inputs, conv_weight, score_weight, lengths, offsets, cotangent):
    rows, pairs, files = inputs.shape[1], cotangent.shape[1], offsets.shape[1]
    shape = jax.ShapeDtypeStruct

    def flip(value, axis):
        return lax.ppermute(value, axis, [(0, 1), (1, 0)])

    def cycle(value, by):
        return lax.ppermute(value, "seq", [(i, (i + by) % SLOTS) for i in range(SLOTS)])

    message = shape((rows + pairs + PAD, HALF), BF)
    mine, other, mw1, mw2, mw3 = call(
        pack_kernel,
        (
            message,
            message,
            shape((HALO_ROW + 2 * PAD * SLOTS + SPARE, GROUP_WIDTH), BF),
            shape((HALO_ROW, GROUP_WIDTH), BF),
            shape((HALO_ROW + 2 * PAD * SLOTS, GROUP_WIDTH), BF),
        ),
        scratch=(
            pltpu.SMEM(offsets.shape, jnp.int32),
            pltpu.VMEM(inputs.shape, BF),
            pltpu.VMEM(cotangent.shape, BF),
            pltpu.VMEM((1, score_weight.shape[0]), BF),
            pltpu.SemaphoreType.DMA((5,)),
        ),
        hbm=5,
    )(*(pltpu.with_memory_space_constraint(v, pltpu.HBM) for v in (offsets, inputs, cotangent, conv_weight, score_weight.reshape(1, -1))), lengths.reshape(1, 1))
    other = flip(other, "dp")
    halo = shape((2 * PAD, HALF), BF)
    kernel_mine, halo_own, halo_other = call(
        join_kernel, (shape((SLOTS * SHARD + JOINED_SPARE, GROUP_WIDTH), BF), halo, halo)
    )(mw2, cycle(mw1, 1), cycle(mw2, 2), cycle(mw3, 3))
    halo_other = flip(halo_other, "dp")
    shards = (kernel_mine, flip(kernel_mine, "fsdp"))
    own_windows = call(
        functools.partial(own_window_kernel, files),
        shape((SLOTS, rows, KERNEL * GROUP_WIDTH), BF),
    )(mine)
    left = shape((2, pairs + PAD, HALF), BF)
    sums = shape((2, 16, GROUP_WIDTH), F32)
    hidden, left_main, partial = call(
        functools.partial(hidden_kernel, files), (shape((2, rows, HALF), F32), left, sums)
    )(own_windows, mine, other, *shards)
    edge_hidden, left, partial = call(
        functools.partial(edge_hidden_kernel, files),
        (shape((2, 2 * PAD, HALF), F32), left, sums),
    )(mine, other, halo_own, halo_other, *shards, left_main, partial)
    partial_r = flip(partial, "dp")
    windows = call(
        functools.partial(window_kernel, files),
        shape((SLOTS, KERNEL * GROUP_WIDTH, 2 * (rows + 2 * PAD)), BF),
        cost=pl.CostEstimate(flops=0, transcendentals=0, bytes_accessed=2 * 1024 * 1024),
    )(mine, other, halo_own, halo_other, partial)
    grad_rows = SLOTS * (SCORE_ROW + PAD)
    hg, hg_ahead, kept, send = call(
        functools.partial(mix_kernel, files),
        (
            shape((2, rows, HALF), BF),
            shape((2, 2 * PAD, HALF), BF),
            shape((grad_rows, GROUP_WIDTH), F32),
            shape((grad_rows, GROUP_WIDTH), F32),
        ),
    )(mine, other, windows, hidden, edge_hidden, left, partial, partial_r)
    got = flip(send, "fsdp")
    x_send = call(functools.partial(send_kernel, files), shape((rows, HALF), BF))(
        hg, hg_ahead, other, *shards
    )
    x_got = flip(x_send, "dp")
    summed = shape((HALO_ROW, GROUP_WIDTH), BF)
    first = shape((HALO_ROW + PAD, GROUP_WIDTH), BF)
    sums = call(add_kernel, tuple(first if j == 2 else summed for j in range(1, SLOTS)))(kept, got)
    final = [cycle(value, -j) for j, value in zip(range(1, SLOTS), sums)]
    vmem, hbm = pl.BlockSpec(memory_space=pltpu.VMEM), pl.BlockSpec(memory_space=pltpu.HBM)
    params = pltpu.CompilerParams(vmem_limit_bytes=48 * 1024 * 1024)
    input_grad = pl.pallas_call(
        functools.partial(own_kernel, files),
        out_shape=shape(inputs.shape, BF),
        in_specs=[vmem] * 5,
        out_specs=hbm,
        scratch_shapes=[pltpu.VMEM((rows, HALF), BF), pltpu.SemaphoreType.DMA((SLOTS,))],
        compiler_params=params,
        cost_estimate=pl.CostEstimate(flops=0, transcendentals=0, bytes_accessed=4 * 1024 * 1024),
    )(hg, hg_ahead, mine, *shards)
    input_grad = pl.pallas_call(
        place_kernel,
        out_shape=shape(inputs.shape, BF),
        in_specs=[vmem, hbm],
        out_specs=hbm,
        scratch_shapes=[pltpu.SemaphoreType.DMA((SLOTS,))],
        input_output_aliases={1: 0},
        compiler_params=params,
    )(x_got, input_grad)
    kernel_grad, score_grad = pl.pallas_call(
        finish_kernel,
        out_shape=(
            shape((SCORE_ROW, GROUP_WIDTH), F32),
            shape((1, GROUP_WIDTH // 2), F32),
        ),
        in_specs=[vmem] * 5,
        out_specs=(hbm, hbm),
        scratch_shapes=[
            pltpu.VMEM((SCORE_ROW, GROUP_WIDTH), F32),
            pltpu.VMEM((1, GROUP_WIDTH // 2), F32),
            pltpu.SemaphoreType.DMA((2,)),
        ],
        compiler_params=params,
    )(kept, got, *final)
    return (input_grad, kernel_grad, score_grad.reshape(-1))


def solution(mesh):
    placed = (
        P(("parts", "dp", "fsdp"), "seq", None),
        P(("seq", "dp", "fsdp"), None),
        P(("seq", "dp", "fsdp")),
        P(("parts", "dp", "fsdp")),
        P(("parts", "dp", "fsdp"), None),
        P(("parts", "dp", "fsdp"), "seq", None),
    )
    paired = mesh.shape["seq"] == SLOTS and mesh.shape["dp"] == 2 and mesh.shape["fsdp"] == 2
    return jax.shard_map(
        per_device_paired if paired else per_device_general,
        mesh=mesh,
        in_specs=placed,
        out_specs=(
            P(("parts", "dp", "fsdp"), "seq", None),
            P(("parts", "seq", "dp", "fsdp"), None),
            P(("parts", "seq", "dp", "fsdp")),
        ),
        check_vma=False,
    )
```
